32 devices in a mesh: dp: 4 (over y, core), code: 8 (over z, x).
Axes of the slice: x: 2, y: 2, z: 4, core: 2. Of those that a mesh axis runs over, the one named last changes fastest.
Arguments:
- cached_keys: bfloat16 [131072, 128], P(('dp', 'code')), may hold values from -128 to 128
- codebook: float32 [65536, 128], P('code'), may hold values from -4 to 4
- block_lists: int32 [256, 6], P(('dp', 'code')), may hold values from 0 to 255, as said below
- counts: int32 [256], P(('dp', 'code')), may hold values from 2 to 6, as said below
Outputs:
- codebook_out: float32 [65536, 128], P('code')
- logsum: float32 [131072], P(('dp', 'code'))
The draws below stay inside these ranges and needn't reach their ends.
Inputs may be any that keep to these rules, and one draw needn't show every extreme that they name: `block_lists`: within a row the first counts entries are distinct; entries past the count repeat the first. Owner o holds blocks o * (256 / the size of code) onward, consecutively; the key blocks of one device (aligned runs of 8 rows) name at most 1 distinct blocks of one owner, and in every draw one owner has exactly 1 named by every device. `counts`: some key block of every device lists 6 blocks.
All inputs are finite; a program needn't handle non-finite values.
Results may differ from the reference program's by a relative error of at most 0.0007.
Values sent between devices are 32-bit elements; how exact they have to be, the bound alone decides.
A program may use at most 64 MiB of HBM per device.

```python
import jax
import jax.numpy as jnp
from jax import lax

H = 128
CODES = 65536
CBLK = 256
BLOCK = 512
LIST_MAX = 6
CAP = 1
ITERS = 2
KB_DEV = 8
KBLOCKS = 256
KEYS = 131072
CBLOCKS = 256
N_CODE = 8


def shared_codebook(key):
    base = jax.random.fold_in(key, 11)
    return jnp.clip(jax.random.normal(base, (CODES, H), jnp.float32), -4.0, 4.0)


def shared_lists(key):
    base = jax.random.fold_in(key, 23)
    device_count = KBLOCKS // KB_DEV
    own_blocks = CODES // CBLK // N_CODE
    width_slots = N_CODE * CAP
    first = jax.random.randint(jax.random.fold_in(base, 1), (device_count, N_CODE), 0, own_blocks)
    stride = jax.random.randint(jax.random.fold_in(base, 2), (device_count, N_CODE), 1, max(own_blocks // CAP, 2))
    local = (first[:, :, None] + jnp.arange(CAP, dtype=jnp.int32)[None, None, :] * stride[:, :, None]) % own_blocks
    owner_ids = jnp.arange(N_CODE, dtype=jnp.int32)[None, :, None]
    block_ids = (owner_ids * own_blocks + local).reshape(device_count, width_slots)
    hot_owner = jax.random.randint(jax.random.fold_in(base, 3), (), 0, N_CODE)
    coin = jax.random.randint(jax.random.fold_in(base, 4), (device_count, N_CODE, CAP), 0, 2)
    slot_pos = jnp.arange(CAP, dtype=jnp.int32)[None, None, :]
    is_hot = owner_ids == hot_owner
    usable = jnp.where((slot_pos == 0) | is_hot, 1, coin).reshape(device_count, width_slots)
    slot_index = jnp.arange(width_slots, dtype=jnp.int32)
    noise = jax.random.randint(jax.random.fold_in(base, 5), (device_count, KB_DEV, width_slots), 0, 1 << 20)
    ranking = noise * width_slots + slot_index[None, None, :]
    ranking = jnp.where(usable[:, None, :] == 1, ranking, -1 - slot_index[None, None, :])
    hot_flat = jnp.broadcast_to(is_hot, (1, N_CODE, CAP)).reshape(1, width_slots)
    first_row = (jnp.arange(KB_DEV, dtype=jnp.int32) == 0)[None, :, None]
    ranking = ranking + jnp.where(first_row & hot_flat[:, None, :], 1 << 28, 0)
    top_slots = lax.top_k(ranking, LIST_MAX)[1]
    picked = jnp.take_along_axis(jnp.broadcast_to(block_ids[:, None, :], (device_count, KB_DEV, width_slots)), top_slots, axis=2)
    counts = jax.random.randint(jax.random.fold_in(base, 6), (device_count, KB_DEV), 2, LIST_MAX + 1)
    counts = jnp.where(jnp.arange(KB_DEV, dtype=jnp.int32)[None, :] == 1, LIST_MAX, counts)
    within = jnp.arange(LIST_MAX, dtype=jnp.int32)[None, None, :] < counts[:, :, None]
    picked = jnp.where(within, picked, picked[:, :, 0:1])
    return (picked.reshape(KBLOCKS, LIST_MAX).astype(jnp.int32), counts.reshape(KBLOCKS).astype(jnp.int32))


def draw_codebook(key, part):
    return shared_codebook(key)


def draw_block_lists(key, part):
    return shared_lists(key)[0]


def draw_counts(key, part):
    return shared_lists(key)[1]


def draw_cached_keys(key, part):
    noise = jnp.clip(jax.random.normal(jax.random.fold_in(key, 13), (KEYS, H), jnp.float32), -4.0, 4.0)
    return noise.astype(jnp.bfloat16)


def setup_inputs(seed: int = 0) -> dict:
    splits = jax.random.split(jax.random.key(seed), 5)
    return {
        "cached_keys": draw_cached_keys(jax.random.fold_in(splits[4], 71), 0),
        "codebook": draw_codebook(jax.random.fold_in(splits[4], 71), 0),
        "block_lists": draw_block_lists(jax.random.fold_in(splits[4], 71), 0),
        "counts": draw_counts(jax.random.fold_in(splits[4], 71), 0),
    }


def reference(cached_keys, codebook, block_lists, counts):
    masked_score = -1e+30
    key_tiles = cached_keys.reshape(-1, BLOCK, H)
    listed_ok = jnp.arange(LIST_MAX)[None, :] < counts[:, None]
    current = codebook
    logsum = None
    for sweep in range(ITERS):
        code_full = current.reshape(CBLOCKS, CBLK, H)
        code_norm = lax.optimization_barrier(jnp.sum(current * current, axis=1)).reshape(CBLOCKS, CBLK)

        def one_block(running, block_item):
            total_sums, total_mass = running
            tile_keys, picked, listed = block_item
            word_rows = code_full[picked].reshape(-1, H)
            word_norms = code_norm[picked].reshape(-1)
            inner = lax.dot_general(tile_keys.astype(jnp.float32), word_rows, (((1,), (1,)), ((), ())), precision=lax.Precision.HIGHEST, preferred_element_type=jnp.float32)
            scores = (inner - 0.5 * word_norms[None, :]) / jnp.sqrt(jnp.float32(H))
            column_live = jnp.repeat(listed, CBLK)
            scores = jnp.where(column_live[None, :], scores, masked_score)
            row_top = lax.optimization_barrier(jnp.max(scores, axis=1, keepdims=True))
            unnorm = jnp.exp(scores - row_top)
            row_total = lax.optimization_barrier(jnp.sum(unnorm, axis=1, keepdims=True))
            row_logsum = row_top[:, 0] + jnp.log(row_total[:, 0])
            posterior = (unnorm / row_total).astype(jnp.bfloat16)
            weighted = lax.dot_general(posterior, tile_keys, (((0,), (0,)), ((), ())), preferred_element_type=jnp.float32)
            weight = lax.optimization_barrier(jnp.sum(posterior.astype(jnp.float32), axis=0))
            total_sums = total_sums.at[picked].add(weighted.reshape(LIST_MAX, CBLK, H))
            total_mass = total_mass.at[picked].add(weight.reshape(LIST_MAX, CBLK))
            return ((total_sums, total_mass), row_logsum)
        start_state = (jnp.zeros((CBLOCKS, CBLK, H), jnp.float32), jnp.zeros((CBLOCKS, CBLK), jnp.float32))
        (total_sums, total_mass), logsum = lax.scan(one_block, start_state, (key_tiles, block_lists, listed_ok))
        current = (total_sums.reshape(CODES, H) + current) / (total_mass.reshape(CODES)[:, None] + 1.0)
    return (current, logsum.reshape(-1))
```

```python
import functools
import math

import jax
import jax.numpy as jnp
from jax import lax
from jax.experimental import pallas as pl
from jax.experimental.pallas import tpu as pltpu
from jax.sharding import PartitionSpec as P

CBLK = 256
LIST_MAX = 6
ITERS = 2
MROWS = 8
MESH = pl.DeviceIdType.MESH
VLIMIT = 60 * 1024 * 1024
HELD_BYTES = 16 * 1024 * 1024

VM = pl.BlockSpec(memory_space=pltpu.VMEM)
SM = pl.BlockSpec(memory_space=pltpu.SMEM)
ANY = pl.BlockSpec(memory_space=pl.ANY)


def flip(value, bits):
    out = value
    bit = 1
    while bit <= bits:
        if bits & bit:
            out = out + bit * (1 - 2 * (value // bit % 2))
        bit *= 2
    return out


def remote(src, dst, send, recv, dp, code):
    return pltpu.make_async_remote_copy(
        src_ref=src, dst_ref=dst, send_sem=send, recv_sem=recv,
        device_id=(dp, code), device_id_type=MESH,
    )


def fetch_kernel(
    n_code, want_ref, book_hbm, out_ref, served_ref, asked_ref,
    book, ids, id_send, id_recv, send_sem, recv_sem, book_sem, own_sem, smem_sem,
):
    d = lax.axis_index("dp")
    o = lax.axis_index("code")
    barrier = pltpu.get_barrier_semaphore()
    for k in range(1, n_code):
        pl.semaphore_signal(barrier, inc=1, device_id=(d, flip(o, k)), device_id_type=MESH)
    load = pltpu.make_async_copy(book_hbm, book, book_sem)
    load.start()
    own = pltpu.make_async_copy(want_ref.at[o], asked_ref.at[o], own_sem)
    own.start()
    pl.semaphore_wait(barrier, n_code - 1)
    asks = []
    for k in range(1, n_code):
        peer = flip(o, k)
        copy = remote(
            want_ref.at[peer], asked_ref.at[o], id_send.at[k], id_recv.at[k], d, peer
        )
        copy.start()
        asks.append(copy)
    load.wait()
    copies = []
    for k in range(1, n_code):
        peer = flip(o, k)
        asks[k - 1].wait_recv()
        move = pltpu.make_async_copy(asked_ref.at[peer], ids.at[k], smem_sem.at[k])
        move.start()
        move.wait()
        served_ref[peer] = book[ids[k, 0, 0]]
        copy = remote(
            served_ref.at[peer], out_ref.at[o], send_sem.at[k], recv_sem.at[k], d, peer
        )
        copy.start()
        copies.append(copy)
    own.wait()
    move = pltpu.make_async_copy(asked_ref.at[o], ids.at[0], smem_sem.at[0])
    move.start()
    move.wait()
    block = book[ids[0, 0, 0]]
    served_ref[o] = block
    out_ref[o] = block
    for ask in asks:
        ask.wait_send()
    for copy in copies:
        copy.wait()


def exchange_kernel(n_dp, n_code, reply, *refs):
    if reply:
        (sums_ref, served_ref, asked_ref, con_ref, back_ref, acc, stage,
         a_send, a_recv, y_send, y_recv, c_send, c_recv, own_sem, b_send, b_recv) = refs
    else:
        (sums_ref, con_ref,
         a_send, a_recv, y_send, y_recv, c_send, c_recv, own_sem) = refs
    d = lax.axis_index("dp")
    o = lax.axis_index("code")
    n_y = n_dp // 2
    y = d // 2
    core = d % 2
    mate = y * 2 + 1 - core
    barrier = pltpu.get_barrier_semaphore()
    for k in range(1, n_code):
        pl.semaphore_signal(barrier, inc=1, device_id=(d, flip(o, k)), device_id_type=MESH)
    for j in range(1, n_y):
        pl.semaphore_signal(
            barrier, inc=1, device_id=((y + j) % n_y * 2 + core, o), device_id_type=MESH
        )
    pl.semaphore_signal(barrier, inc=1, device_id=(mate, o), device_id_type=MESH)
    own = pltpu.make_async_copy(sums_ref.at[o], con_ref.at[d * n_code + o], own_sem)
    own.start()
    pl.semaphore_wait(barrier, n_code - 1 + n_y - 1 + 1)

    sends = []
    across = []
    for k in range(1, n_code):
        peer = flip(o, k)
        copy = remote(
            sums_ref.at[peer], con_ref.at[d * n_code + o], a_send.at[k], a_recv.at[k], d, peer
        )
        copy.start()
        across.append(copy)
        sends.append(copy)

    def to_y(k, j):
        row = d * n_code + flip(o, k)
        return remote(
            con_ref.at[row], con_ref.at[row], y_send.at[j, k], y_recv.at[j, k],
            (y + j) % n_y * 2 + core, o,
        )

    def held(k, j):
        return ((y + n_y - j) % n_y * 2 + core) * n_code + flip(o, k)

    def to_mate(k, j):
        row = held(k, j)
        return remote(
            con_ref.at[row], con_ref.at[row], c_send.at[j, k], c_recv.at[j, k], mate, o
        )

    if reply:
        acc[...] = jnp.zeros_like(acc)

    def absorb(row):
        if not reply:
            return
        here = con_ref[row, pl.ds(CBLK + 2, 1), :]

        def one(i, c):
            same = (asked_ref[i, pl.ds(0, 1), :].astype(jnp.float32) == here).astype(jnp.float32)
            acc[i] += con_ref[row] * same
            return c

        lax.fori_loop(0, n_code, one, 0)

    y_copies = {}
    mates = {}
    for k in range(n_code):
        if k == 0:
            own.wait()
        else:
            across[k - 1].wait_recv()
        for j in range(1, n_y):
            copy = to_y(k, j)
            copy.start()
            y_copies[j, k] = copy
            sends.append(copy)
        copy = to_mate(k, 0)
        copy.start()
        mates[0, k] = copy
        sends.append(copy)
        absorb(held(k, 0))
    for k in range(n_code):
        for j in range(1, n_y):
            y_copies[j, k].wait_recv()
            copy = to_mate(k, j)
            copy.start()
            mates[j, k] = copy
            sends.append(copy)
            absorb(held(k, j))
        mates[0, k].wait_recv()
        absorb(held(k, 0) + (1 - 2 * core) * n_code)
    for k in range(n_code):
        for j in range(1, n_y):
            mates[j, k].wait_recv()
            absorb(held(k, j) + (1 - 2 * core) * n_code)
    if reply:
        backs = []
        for k in range(n_code):
            peer = flip(o, k)
            for h in range(2):
                inv = 1.0 / (acc[peer, pl.ds(CBLK + h, 1), :] + 1.0)
                column = jnp.transpose(jnp.broadcast_to(inv, (128, 128)))
                rows = pl.ds(h * 128, 128)
                fresh = (acc[peer, rows, :] + served_ref[peer, rows, :]) * column
                if k == 0:
                    back_ref[o, rows, :] = fresh
                else:
                    stage[k, rows, :] = fresh
        for k in range(n_code - 1, 0, -1):
            copy = remote(
                stage.at[k], back_ref.at[o], b_send.at[k], b_recv.at[k], d, flip(o, k)
            )
            copy.start()
            backs.append(copy)
        for copy in backs:
            copy.wait()
    for copy in sends:
        copy.wait_send()


def sweeps_kernel(n_dp, n_code, key_blocks, block, own_blocks, feature, sweeps, *refs):
    slots_ref, counts_ref, want_ref, keys_ref, book_hbm = refs[:5]
    con_refs = refs[5 : 5 + sweeps]
    logsum_ref = refs[5 + sweeps]
    (unnorm, peaks, totals, words, norms, kst, kext, sums, acc, stage, served,
     fetched, back, asked, part, less, ids,
     id_send, id_recv, f_send, f_recv, b_send, b_recv,
     a_send, a_recv, y_send, y_recv, c_send, c_recv,
     book_sem, own_sem, smem_sem) = refs[6 + sweeps :]
    scale = math.log2(math.e) / math.sqrt(feature)
    keys = key_blocks * block
    chunks = keys // 128
    d = lax.axis_index("dp")
    o = lax.axis_index("code")
    n_y = n_dp // 2
    y = d // 2
    core = d % 2
    mate = y * 2 + 1 - core
    far = n_code // 2

    def turn(k):
        out = o
        bit = 1
        while bit < n_code:
            out = out + bit * (k // bit % 2) * (1 - 2 * (o // bit % 2))
            bit *= 2
        return out

    barrier = pltpu.get_barrier_semaphore()
    for k in range(1, n_code):
        pl.semaphore_signal(barrier, inc=1, device_id=(d, flip(o, k)), device_id_type=MESH)
    for j in range(1, n_y):
        pl.semaphore_signal(
            barrier, inc=1, device_id=((y + j) % n_y * 2 + core, o), device_id_type=MESH
        )
    pl.semaphore_signal(barrier, inc=1, device_id=(mate, o), device_id_type=MESH)

    book = unnorm.at[n_code - 1]
    load = pltpu.make_async_copy(book_hbm, book.at[pl.ds(0, own_blocks)], book_sem)
    load.start()
    asked[0] = want_ref[o]
    own = pltpu.make_async_copy(want_ref.at[o], ids.at[0], smem_sem.at[0])
    own.start()
    pl.semaphore_wait(barrier, n_code - 1 + n_y - 1 + 1)

    asks = []
    for k in range(1, n_code):
        peer = flip(o, k)
        copy = remote(want_ref.at[peer], asked.at[k], id_send.at[k], id_recv.at[k], d, peer)
        copy.start()
        asks.append(copy)

    def gate(kb, c):
        count = counts_ref[kb]
        for k in range(n_code):
            slot = turn(k)
            hit = jnp.float32(1e30)
            for l in range(LIST_MAX):
                same = (slots_ref[kb, l] == slot) & (count > l)
                hit = jnp.where(same, jnp.float32(0.0), hit)
            less[kb, k] = hit
        return c

    def serve_copy(k):
        peer = flip(o, k)
        return remote(served.at[k], fetched.at[k], f_send.at[k], f_recv.at[k], d, peer)

    def move(k):
        return pltpu.make_async_copy(asked.at[k], ids.at[k], smem_sem.at[k])

    load.wait()
    own.wait()
    first = unnorm[n_code - 1, ids[0, 0, 0]]
    served[0] = first
    fetched[0] = first
    serves = []
    for k in range(1, n_code + 1):
        if k < n_code:
            asks[k - 1].wait_recv()
            move(k).start()
        if k > 1:
            move(k - 1).wait()
            served[k - 1] = unnorm[n_code - 1, ids[k - 1, 0, 0]]
            copy = serve_copy(k - 1)
            copy.start()
            serves.append(copy)

    kext[:, 128:256] = jnp.ones((keys, 128), jnp.bfloat16)
    kext[:, 0:128] = keys_ref[...]

    def turn_keys(c, carry):
        at = pl.ds(pl.multiple_of(c * block, block), block)
        turned = jnp.transpose(keys_ref[at, :])
        kst[0:128, at] = turned
        kst[128:256, at] = turned
        return carry

    lax.fori_loop(0, key_blocks, turn_keys, 0)
    lax.fori_loop(0, key_blocks, gate, 0)

    def score(k, blocks):
        value = blocks[k]
        scaled = value * scale
        hi = scaled.astype(jnp.bfloat16)
        words[:, 0:128] = hi
        words[:, 128:256] = (scaled - hi.astype(jnp.float32)).astype(jnp.bfloat16)
        half = (0.5 * scale) * jnp.sum(value * value, axis=1, keepdims=True)
        norms[...] = jnp.broadcast_to(half, (CBLK, 128))

        def some(i, c):
            for u in range(8):
                q = i * 8 + u
                cols = pl.ds(pl.multiple_of(q * 256, 256), 256)
                right = kst[:, cols]
                for h in range(2):
                    rows = slice(h * 128, (h + 1) * 128)
                    raw = jnp.dot(words[rows, :], right, preferred_element_type=jnp.float32)
                    s = raw - jnp.tile(norms[rows, :], (1, 2))
                    s = s.reshape(16, 8, 256)
                    top = jnp.max(s, axis=0)
                    e = jnp.exp2(s - top[None])
                    peaks[k, h, :, cols] = top
                    totals[k, h, :, cols] = jnp.sum(e, axis=0)
                    e = e.reshape(128, 256)
                    unnorm[k, 2 * q, rows, :] = e[:, 0:128]
                    unnorm[k, 2 * q + 1, rows, :] = e[:, 128:256]
            return c

        lax.fori_loop(0, keys // 256 // 8, some, 0)

    def normalise(last):
        def one(kb, c):
            cols = pl.ds(pl.multiple_of(kb * block, block), block)
            top = jnp.full((8, block), -3e38, jnp.float32)
            for k in range(n_code):
                for h in range(2):
                    top = jnp.maximum(top, peaks[k, h, :, cols] - less[kb, k])
            peak = jnp.max(top, axis=0, keepdims=True)
            total = jnp.zeros((8, block), jnp.float32)
            for k in range(n_code):
                for h in range(2):
                    w = jnp.exp2((peaks[k, h, :, cols] - less[kb, k]) - peak)
                    total = total + w * totals[k, h, :, cols]
                    peaks[k, h, :, cols] = w
            total = jnp.sum(total, axis=0, keepdims=True)
            if last:
                logsum_ref[kb] = peak * math.log(2.0) + jnp.log(total)
            inv = 1.0 / total
            for k in range(n_code):
                for h in range(2):
                    peaks[k, h, :, cols] = peaks[k, h, :, cols] * inv
            return c

        lax.fori_loop(0, key_blocks, one, 0)

    def collect(k):
        total = None
        for q in range(keys // 512):
            halves = []
            for h in range(2):
                rows = slice(h * 128, (h + 1) * 128)
                tiles = []
                for u in range(4):
                    e = unnorm[k, q * 4 + u, rows, :].reshape(16, 8, 128)
                    w = peaks[k, h, :, pl.ds((q * 4 + u) * 128, 128)]
                    tiles.append((e * w[None]).reshape(128, 128).astype(jnp.bfloat16))
                halves.append(jnp.concatenate(tiles, axis=1))
            piece = jnp.dot(
                jnp.concatenate(halves, axis=0), kext[q * 512 : (q + 1) * 512, :],
                preferred_element_type=jnp.float32,
            )
            total = piece if total is None else total + piece
        part[...] = total
        for h in range(2):
            turned = jnp.transpose(part[h * 128 : (h + 1) * 128, 128:256])
            sums[k, CBLK + h : CBLK + h + 1, :] = turned[0:1, :]
        sums[k, CBLK + 2 :, :] = want_ref[turn(k), 2:, :].astype(jnp.float32)
        sums[k, :CBLK, :] = part[:, 0:128]

    def held(k, j):
        return ((y + n_y - j) % n_y * 2 + core) * n_code + flip(o, k)

    order = list(range(1, n_code)) + [0]
    backs = []
    for sweep in range(sweeps):
        reply = sweep + 1 < sweeps
        con_ref = con_refs[sweep]
        blocks = fetched if sweep == 0 else back

        def scoring(k, c):
            @pl.when(k > 0)
            def _():
                if sweep == 0:
                    serve_copy_at(k).wait_recv()
                else:
                    back_copy_at(k).wait_recv()

            score(k, blocks)
            return c

        def serve_copy_at(k):
            return remote(served.at[k], fetched.at[k], f_send.at[k], f_recv.at[k], d, turn(k))

        def back_copy_at(k):
            return remote(stage.at[k], back.at[k], b_send.at[k], b_recv.at[k], d, turn(k))

        lax.fori_loop(0, n_code, scoring, 0)
        normalise(not reply)

        def across(k):
            return remote(
                sums.at[k], con_ref.at[d * n_code + o],
                a_send.at[sweep, k], a_recv.at[sweep, k], d, turn(k),
            )

        collect(far)

        def step(k, c):
            collect(k)
            across(k - 1).start()
            return c

        lax.fori_loop(far + 1, n_code, step, 0)
        collect(0)
        across(n_code - 1).start()
        mine = pltpu.make_async_copy(sums.at[0], con_ref.at[d * n_code + o], own_sem)
        mine.start()

        sends = []

        def to_y(k, j):
            row = held(k, 0)
            copy = remote(
                con_ref.at[row], con_ref.at[row],
                y_send.at[sweep, j, k], y_recv.at[sweep, j, k],
                (y + j) % n_y * 2 + core, o,
            )
            copy.start()
            sends.append(copy)
            return copy

        def to_mate(k, j):
            row = held(k, j)
            copy = remote(
                con_ref.at[row], con_ref.at[row],
                c_send.at[sweep, j, k], c_recv.at[sweep, j, k], mate, o,
            )
            copy.start()
            sends.append(copy)
            return copy

        if reply:
            acc[...] = jnp.zeros_like(acc)

        def absorb(row):
            if not reply:
                return
            here = con_ref[row, pl.ds(CBLK + 2, 1), :]

            def one(i, c):
                same = (asked[i, pl.ds(0, 1), :].astype(jnp.float32) == here).astype(jnp.float32)
                acc[i] += con_ref[row] * same
                return c

            lax.fori_loop(0, n_code, one, 0)

        y_copies = {}
        mates = {}
        mine.wait()
        for j in range(1, n_y):
            y_copies[j, 0] = to_y(0, j)
        mates[0, 0] = to_mate(0, 0)

        def near(k, c):
            collect(k)

            @pl.when(k > 1)
            def _():
                across(k - 1).start()

            return c

        lax.fori_loop(1, far, near, 0)
        absorb(held(0, 0))
        across(far - 1).start()

        for k in range(1, n_code):
            across(k).wait_recv()
            for j in range(1, n_y):
                y_copies[j, k] = to_y(k, j)
            mates[0, k] = to_mate(k, 0)
            absorb(held(k, 0))
        for k in range(n_code):
            for j in range(1, n_y):
                y_copies[j, k].wait_recv()
                mates[j, k] = to_mate(k, j)
                absorb(held(k, j))
            mates[0, k].wait_recv()
            absorb(held(k, 0) + (1 - 2 * core) * n_code)
        for k in range(n_code):
            for j in range(1, n_y):
                mates[j, k].wait_recv()
                absorb(held(k, j) + (1 - 2 * core) * n_code)
        if reply:
            for at, k in enumerate(order):
                for h in range(2):
                    inv = 1.0 / (acc[k, pl.ds(CBLK + h, 1), :] + 1.0)
                    column = jnp.transpose(jnp.broadcast_to(inv, (128, 128)))
                    rows = pl.ds(h * 128, 128)
                    fresh = (acc[k, rows, :] + served[k, rows, :]) * column
                    if k == 0:
                        back[0, rows, :] = fresh
                    else:
                        stage[k, rows, :] = fresh
                if at > 0:
                    copy = back_copy_at(order[at - 1])
                    copy.start()
                    backs.append(copy)
        for k in range(1, n_code):
            across(k).wait_send()
        for copy in sends:
            copy.wait_send()
    for copy in asks + serves + backs:
        copy.wait_send()


def finish_kernel(n, own_blocks, sweeps, *refs):
    con_hbm = refs[:sweeps]
    book_hbm, out_hbm = refs[sweeps : sweeps + 2]
    con, total, mass, ids, con_sem, book_sem, out_sem = refs[sweeps + 2 :]
    book = pltpu.make_async_copy(book_hbm, total, book_sem)
    book.start()
    half = n // 2

    def load(t, h):
        rows = pl.ds(h * half, half)
        return pltpu.make_async_copy(con_hbm[t].at[rows], con.at[rows], con_sem.at[h])

    load(0, 0).start()
    load(0, 1).start()
    outs = []
    for t in range(sweeps):
        mass[...] = jnp.ones_like(mass)
        for h in range(2):
            load(t, h).wait()
            if t == 0:

                def name(j, c):
                    for u in range(4):
                        i = j * 4 + u
                        ids[i] = jnp.max(con[i, pl.ds(CBLK + 2, 1), :]).astype(jnp.int32)
                    return c

                lax.fori_loop(h * half // 4, (h + 1) * half // 4, name, 0)
                if h == 0:
                    book.wait()

            def add(j, c):
                b = ids[j]
                total[b] += con[j, :CBLK, :]
                for g in range(2):
                    row = pl.ds(g * (mass.shape[0] // 2) + b, 1)
                    mass[row, :] += con[j, pl.ds(CBLK + g, 1), :]
                return c

            lax.fori_loop(h * half, (h + 1) * half, add, 0)
            if t + 1 < sweeps:
                load(t + 1, h).start()
        columns = jnp.transpose(1.0 / mass[...])
        for b in range(own_blocks):
            for g in range(2):
                lane = g * (mass.shape[0] // 2) + b
                total[b, g * 128 : (g + 1) * 128, :] = (
                    total[b, g * 128 : (g + 1) * 128, :] * columns[:, lane : lane + 1]
                )
            if t + 1 == sweeps:
                out = pltpu.make_async_copy(total.at[b], out_hbm.at[b], out_sem.at[b])
                out.start()
                outs.append(out)
    for out in outs:
        out.wait()


def assign_kernel(
    n_slots, key_blocks, block, feature,
    slots_ref, counts_ref, fetched_ref, keys_ref, want_ref,
    sums_ref, logsum_ref,
    words, norms, kst, kext, picked, scores, post, acc,
):
    scale = math.log2(math.e) / math.sqrt(feature)

    for s in range(n_slots):
        value = fetched_ref[s]
        scaled = value * scale
        hi = scaled.astype(jnp.bfloat16)
        words[s, :, 0:128] = hi
        words[s, :, 128:256] = (scaled - hi.astype(jnp.float32)).astype(jnp.bfloat16)
        half = (0.5 * scale) * jnp.sum(value * value, axis=1, keepdims=True)
        norms[s] = jnp.broadcast_to(half, (CBLK, 128))
        acc[s] = jnp.zeros((CBLK, 256), jnp.float32)
    kext[:, 128:256] = jnp.ones((block, 128), jnp.bfloat16)

    def key_block(kb, c):
        keys = keys_ref[pl.ds(pl.multiple_of(kb * block, block), block), :]
        kext[:, 0:128] = keys
        turned = jnp.transpose(keys)
        kst[0:128, :] = turned
        kst[128:256, :] = turned
        count = counts_ref[kb]
        slots = [slots_ref[kb, l] for l in range(LIST_MAX)]
        for l in range(LIST_MAX):
            picked[l * CBLK : (l + 1) * CBLK, :] = words[slots[l]]
        raw = jnp.dot(picked[...], kst[...], preferred_element_type=jnp.float32)
        top = jnp.full((8, block), -3e38, jnp.float32)
        for l in range(LIST_MAX):
            rows = slice(l * CBLK, (l + 1) * CBLK)
            less = norms[slots[l]] + jnp.where(l < count, 0.0, 1e30)
            s = raw[rows] - jnp.tile(less, (1, block // 128))
            scores[rows, :] = s
            top = jnp.maximum(top, jnp.max(s.reshape(CBLK // 8, 8, block), axis=0))
        peak = jnp.max(top, axis=0, keepdims=True)
        total = jnp.zeros((8, block), jnp.float32)
        for l in range(LIST_MAX):
            rows = slice(l * CBLK, (l + 1) * CBLK)
            e = jnp.exp2(scores[rows, :] - peak)
            scores[rows, :] = e
            total = total + jnp.sum(e.reshape(CBLK // 8, 8, block), axis=0)
        total = jnp.sum(total, axis=0, keepdims=True)
        logsum_ref[kb] = peak * math.log(2.0) + jnp.log(total)
        inv = 1.0 / total
        post[...] = (scores[...] * inv).astype(jnp.bfloat16)
        weighted = jnp.dot(post[...], kext[...], preferred_element_type=jnp.float32)
        for l in range(LIST_MAX):
            acc[slots[l]] += weighted[l * CBLK : (l + 1) * CBLK]
        return c

    lax.fori_loop(0, key_blocks, key_block, 0)

    for s in range(n_slots):
        sums_ref[s, :CBLK, :] = acc[s, :, 0:128]
        for h in range(2):
            turned = jnp.transpose(acc[s, h * 128 : (h + 1) * 128, 128:256])
            sums_ref[s, CBLK + h : CBLK + h + 1, :] = turned[0:1, :]
        sums_ref[s, CBLK + 2 :, :] = want_ref[s, 2:, :].astype(jnp.float32)


def on_device(cached_keys, codebook, block_lists, counts):
    n_dp = lax.axis_size("dp")
    n_code = lax.axis_size("code")
    n = n_dp * n_code
    own_rows, feature = codebook.shape
    own_blocks = own_rows // CBLK
    key_blocks = block_lists.shape[0]
    block = cached_keys.shape[0] // key_blocks
    f32 = jnp.float32
    dma = pltpu.SemaphoreType.DMA

    slots = block_lists // own_blocks
    local = block_lists % own_blocks
    wanted = jnp.max(
        jnp.where(
            slots.reshape(-1)[:, None] == jnp.arange(128)[None, :], local.reshape(-1)[:, None], 0
        ),
        axis=0,
    )
    want = jnp.broadcast_to(wanted[:n_code, None, None], (n_code, 8, 128)).astype(jnp.int32)
    blocks = jax.ShapeDtypeStruct((n_code, CBLK, feature), f32)
    sums_shape = jax.ShapeDtypeStruct((n_code, CBLK + MROWS, feature), f32)
    con_shape = jax.ShapeDtypeStruct((n, CBLK + MROWS, feature), f32)
    n_y = n_dp // 2

    def params(**kw):
        return pltpu.CompilerParams(vmem_limit_bytes=VLIMIT, **kw)

    book = codebook.reshape(own_blocks, CBLK, feature)

    def finish(parts, held):
        return pl.pallas_call(
            functools.partial(finish_kernel, n, own_blocks, len(parts)),
            out_shape=jax.ShapeDtypeStruct((own_blocks, CBLK, feature), f32),
            in_specs=[ANY] * (len(parts) + 1),
            out_specs=ANY,
            scratch_shapes=[
                pltpu.VMEM(con_shape.shape, f32),
                pltpu.VMEM((own_blocks, CBLK, feature), f32),
                pltpu.VMEM((max(128, 2 * own_blocks), 128), f32),
                pltpu.SMEM((n,), jnp.int32),
                dma((2,)), dma, dma((own_blocks,)),
            ],
            compiler_params=params(),
        )(*parts, held)

    keys = key_blocks * block
    joint = (
        ITERS * n * (CBLK + MROWS) * feature * 4 <= HELD_BYTES
        and own_blocks * 128 <= keys
        and n_code * CBLK * keys * 4 <= HELD_BYTES * 2 + HELD_BYTES // 2
        and keys % 2048 == 0 and block % 512 == 0
    )
    if joint:
        bf16 = jnp.bfloat16
        results = pl.pallas_call(
            functools.partial(
                sweeps_kernel, n_dp, n_code, key_blocks, block, own_blocks, feature, ITERS
            ),
            out_shape=(con_shape,) * ITERS
            + (jax.ShapeDtypeStruct((key_blocks, 1, block), f32),),
            in_specs=[SM, SM, VM, VM, ANY],
            out_specs=(VM,) * (ITERS + 1),
            scratch_shapes=[
                pltpu.VMEM((n_code, keys // 128, CBLK, 128), f32),
                pltpu.VMEM((n_code, 2, 8, keys), f32),
                pltpu.VMEM((n_code, 2, 8, keys), f32),
                pltpu.VMEM((CBLK, 256), bf16),
                pltpu.VMEM((CBLK, 128), f32),
                pltpu.VMEM((256, keys), bf16),
                pltpu.VMEM((keys, 256), bf16),
                pltpu.VMEM(sums_shape.shape, f32),
                pltpu.VMEM(sums_shape.shape, f32),
                pltpu.VMEM(blocks.shape, f32),
                pltpu.VMEM(blocks.shape, f32),
                pltpu.VMEM(blocks.shape, f32),
                pltpu.VMEM(blocks.shape, f32),
                pltpu.VMEM((n_code, 8, 128), jnp.int32),
                pltpu.VMEM((CBLK, 256), f32),
                pltpu.SMEM((key_blocks, n_code), f32),
                pltpu.SMEM((n_code, 8, 128), jnp.int32),
                dma((n_code,)), dma((n_code,)),
                dma((n_code,)), dma((n_code,)),
                dma((n_code,)), dma((n_code,)),
                dma((ITERS, n_code)), dma((ITERS, n_code)),
                dma((ITERS, n_y, n_code)), dma((ITERS, n_y, n_code)),
                dma((ITERS, n_y, n_code)), dma((ITERS, n_y, n_code)),
                dma, dma, dma((n_code,)),
            ],
            compiler_params=params(collective_id=0, has_side_effects=True),
        )(slots, counts, want, cached_keys, book)
        current = finish(results[:ITERS], book)
        return (current.reshape(own_rows, feature), results[ITERS].reshape(-1))

    fetched, served, asked = pl.pallas_call(
        functools.partial(fetch_kernel, n_code),
        out_shape=(blocks, blocks, jax.ShapeDtypeStruct((n_code, 8, 128), jnp.int32)),
        in_specs=[VM, ANY],
        out_specs=(VM, VM, VM),
        scratch_shapes=[
            pltpu.VMEM((own_blocks, CBLK, feature), f32),
            pltpu.SMEM((n_code, 8, 128), jnp.int32),
            dma((n_code,)), dma((n_code,)), dma((n_code,)), dma((n_code,)),
            dma, dma, dma((n_code,)),
        ],
        compiler_params=params(collective_id=0, has_side_effects=True),
    )(want, book)
    current = book
    for sweep in range(ITERS):
        reply = sweep + 1 < ITERS
        sems = [
            dma((n_code,)), dma((n_code,)),
            dma((n_y, n_code)), dma((n_y, n_code)),
            dma((n_y, n_code)), dma((n_y, n_code)),
            dma,
        ]
        sums, logsum = pl.pallas_call(
            functools.partial(assign_kernel, n_code, key_blocks, block, feature),
            out_shape=(sums_shape, jax.ShapeDtypeStruct((key_blocks, 1, block), f32)),
            in_specs=[SM, SM, VM, VM, VM],
            out_specs=(VM, VM),
            scratch_shapes=[
                pltpu.VMEM((n_code, CBLK, 256), jnp.bfloat16),
                pltpu.VMEM((n_code, CBLK, 128), f32),
                pltpu.VMEM((256, block), jnp.bfloat16),
                pltpu.VMEM((block, 256), jnp.bfloat16),
                pltpu.VMEM((LIST_MAX * CBLK, 256), jnp.bfloat16),
                pltpu.VMEM((LIST_MAX * CBLK, block), f32),
                pltpu.VMEM((LIST_MAX * CBLK, block), jnp.bfloat16),
                pltpu.VMEM((n_code, CBLK, 256), f32),
            ],
            compiler_params=params(),
        )(slots, counts, fetched, cached_keys, want)
        if reply:
            con, fetched = pl.pallas_call(
                functools.partial(exchange_kernel, n_dp, n_code, True),
                out_shape=(con_shape, blocks),
                in_specs=[VM, VM, VM],
                out_specs=(VM, VM),
                scratch_shapes=[
                    pltpu.VMEM(sums_shape.shape, f32), pltpu.VMEM(blocks.shape, f32)
                ] + sems + [dma((n_code,)), dma((n_code,))],
                compiler_params=params(collective_id=1 + sweep, has_side_effects=True),
            )(sums, served, asked)
        else:
            con = pl.pallas_call(
                functools.partial(exchange_kernel, n_dp, n_code, False),
                out_shape=con_shape,
                in_specs=[VM],
                out_specs=VM,
                scratch_shapes=sems,
                compiler_params=params(collective_id=1 + sweep, has_side_effects=True),
            )(sums)
        current = finish([con], current)
        if reply:
            current, fetched = lax.optimization_barrier((current, fetched))
    return (current.reshape(own_rows, feature), logsum.reshape(-1))


def solution(mesh):
    in_specs = (
        P(("dp", "code"), None),
        P("code", None),
        P(("dp", "code"), None),
        P(("dp", "code")),
    )
    out_specs = (P("code", None), P(("dp", "code")))
    return jax.shard_map(
        on_device, mesh=mesh, in_specs=in_specs, out_specs=out_specs, check_vma=False
    )
```

```python
import functools
import math

import jax
import jax.numpy as jnp
from jax import lax
from jax.experimental import pallas as pl
from jax.experimental.pallas import tpu as pltpu
from jax.sharding import PartitionSpec as P

CBLK = 256
LIST_MAX = 6
ITERS = 2
MROWS = 8
MESH = pl.DeviceIdType.MESH
VLIMIT = 60 * 1024 * 1024
HELD_BYTES = 16 * 1024 * 1024

VM = pl.BlockSpec(memory_space=pltpu.VMEM)
SM = pl.BlockSpec(memory_space=pltpu.SMEM)
ANY = pl.BlockSpec(memory_space=pl.ANY)


def flip(value, bits):
    out = value
    bit = 1
    while bit <= bits:
        if bits & bit:
            out = out + bit * (1 - 2 * (value // bit % 2))
        bit *= 2
    return out


def remote(src, dst, send, recv, dp, code):
    return pltpu.make_async_remote_copy(
        src_ref=src, dst_ref=dst, send_sem=send, recv_sem=recv,
        device_id=(dp, code), device_id_type=MESH,
    )


def fetch_kernel(
    n_code, want_ref, book_hbm, out_ref, served_ref, asked_ref,
    book, ids, id_send, id_recv, send_sem, recv_sem, book_sem, own_sem, smem_sem,
):
    d = lax.axis_index("dp")
    o = lax.axis_index("code")
    barrier = pltpu.get_barrier_semaphore()
    for k in range(1, n_code):
        pl.semaphore_signal(barrier, inc=1, device_id=(d, flip(o, k)), device_id_type=MESH)
    load = pltpu.make_async_copy(book_hbm, book, book_sem)
    load.start()
    own = pltpu.make_async_copy(want_ref.at[o], asked_ref.at[o], own_sem)
    own.start()
    pl.semaphore_wait(barrier, n_code - 1)
    asks = []
    for k in range(1, n_code):
        peer = flip(o, k)
        copy = remote(
            want_ref.at[peer], asked_ref.at[o], id_send.at[k], id_recv.at[k], d, peer
        )
        copy.start()
        asks.append(copy)
    load.wait()
    copies = []
    for k in range(1, n_code):
        peer = flip(o, k)
        asks[k - 1].wait_recv()
        move = pltpu.make_async_copy(asked_ref.at[peer], ids.at[k], smem_sem.at[k])
        move.start()
        move.wait()
        served_ref[peer] = book[ids[k, 0, 0]]
        copy = remote(
            served_ref.at[peer], out_ref.at[o], send_sem.at[k], recv_sem.at[k], d, peer
        )
        copy.start()
        copies.append(copy)
    own.wait()
    move = pltpu.make_async_copy(asked_ref.at[o], ids.at[0], smem_sem.at[0])
    move.start()
    move.wait()
    block = book[ids[0, 0, 0]]
    served_ref[o] = block
    out_ref[o] = block
    for ask in asks:
        ask.wait_send()
    for copy in copies:
        copy.wait()


def exchange_kernel(n_dp, n_code, reply, *refs):
    if reply:
        (sums_ref, served_ref, asked_ref, con_ref, back_ref, acc, stage,
         a_send, a_recv, y_send, y_recv, c_send, c_recv, own_sem, b_send, b_recv) = refs
    else:
        (sums_ref, con_ref,
         a_send, a_recv, y_send, y_recv, c_send, c_recv, own_sem) = refs
    d = lax.axis_index("dp")
    o = lax.axis_index("code")
    n_y = n_dp // 2
    y = d // 2
    core = d % 2
    mate = y * 2 + 1 - core
    barrier = pltpu.get_barrier_semaphore()
    for k in range(1, n_code):
        pl.semaphore_signal(barrier, inc=1, device_id=(d, flip(o, k)), device_id_type=MESH)
    for j in range(1, n_y):
        pl.semaphore_signal(
            barrier, inc=1, device_id=((y + j) % n_y * 2 + core, o), device_id_type=MESH
        )
    pl.semaphore_signal(barrier, inc=1, device_id=(mate, o), device_id_type=MESH)
    own = pltpu.make_async_copy(sums_ref.at[o], con_ref.at[d * n_code + o], own_sem)
    own.start()
    pl.semaphore_wait(barrier, n_code - 1 + n_y - 1 + 1)

    sends = []
    across = []
    for k in range(1, n_code):
        peer = flip(o, k)
        copy = remote(
            sums_ref.at[peer], con_ref.at[d * n_code + o], a_send.at[k], a_recv.at[k], d, peer
        )
        copy.start()
        across.append(copy)
        sends.append(copy)

    def to_y(k, j):
        row = d * n_code + flip(o, k)
        return remote(
            con_ref.at[row], con_ref.at[row], y_send.at[j, k], y_recv.at[j, k],
            (y + j) % n_y * 2 + core, o,
        )

    def held(k, j):
        return ((y + n_y - j) % n_y * 2 + core) * n_code + flip(o, k)

    def to_mate(k, j):
        row = held(k, j)
        return remote(
            con_ref.at[row], con_ref.at[row], c_send.at[j, k], c_recv.at[j, k], mate, o
        )

    if reply:
        acc[...] = jnp.zeros_like(acc)

    def absorb(row):
        if not reply:
            return
        here = con_ref[row, pl.ds(CBLK + 2, 1), :]

        def one(i, c):
            same = (asked_ref[i, pl.ds(0, 1), :].astype(jnp.float32) == here).astype(jnp.float32)
            acc[i] += con_ref[row] * same
            return c

        lax.fori_loop(0, n_code, one, 0)

    y_copies = {}
    mates = {}
    for k in range(n_code):
        if k == 0:
            own.wait()
        else:
            across[k - 1].wait_recv()
        for j in range(1, n_y):
            copy = to_y(k, j)
            copy.start()
            y_copies[j, k] = copy
            sends.append(copy)
        copy = to_mate(k, 0)
        copy.start()
        mates[0, k] = copy
        sends.append(copy)
        absorb(held(k, 0))
    for k in range(n_code):
        for j in range(1, n_y):
            y_copies[j, k].wait_recv()
            copy = to_mate(k, j)
            copy.start()
            mates[j, k] = copy
            sends.append(copy)
            absorb(held(k, j))
        mates[0, k].wait_recv()
        absorb(held(k, 0) + (1 - 2 * core) * n_code)
    for k in range(n_code):
        for j in range(1, n_y):
            mates[j, k].wait_recv()
            absorb(held(k, j) + (1 - 2 * core) * n_code)
    if reply:
        backs = []
        for k in range(n_code):
            peer = flip(o, k)
            for h in range(2):
                inv = 1.0 / (acc[peer, pl.ds(CBLK + h, 1), :] + 1.0)
                column = jnp.transpose(jnp.broadcast_to(inv, (128, 128)))
                rows = pl.ds(h * 128, 128)
                fresh = (acc[peer, rows, :] + served_ref[peer, rows, :]) * column
                if k == 0:
                    back_ref[o, rows, :] = fresh
                else:
                    stage[k, rows, :] = fresh
        for k in range(n_code - 1, 0, -1):
            copy = remote(
                stage.at[k], back_ref.at[o], b_send.at[k], b_recv.at[k], d, flip(o, k)
            )
            copy.start()
            backs.append(copy)
        for copy in backs:
            copy.wait()
    for copy in sends:
        copy.wait_send()


def sweeps_kernel(n_dp, n_code, key_blocks, block, own_blocks, feature, sweeps, *refs):
    slots_ref, counts_ref, want_ref, keys_ref, book_hbm = refs[:5]
    con_refs = refs[5 : 5 + sweeps]
    logsum_ref = refs[5 + sweeps]
    (unnorm, peaks, totals, words, norms, kst, kext, sums, acc, stage, served,
     fetched, back, asked, part, less, ids,
     id_send, id_recv, f_send, f_recv, b_send, b_recv,
     a_send, a_recv, y_send, y_recv, c_send, c_recv,
     book_sem, own_sem, smem_sem) = refs[6 + sweeps :]
    scale = math.log2(math.e) / math.sqrt(feature)
    keys = key_blocks * block
    chunks = keys // 128
    d = lax.axis_index("dp")
    o = lax.axis_index("code")
    n_y = n_dp // 2
    y = d // 2
    core = d % 2
    mate = y * 2 + 1 - core
    far = n_code // 2

    def turn(k):
        out = o
        bit = 1
        while bit < n_code:
            out = out + bit * (k // bit % 2) * (1 - 2 * (o // bit % 2))
            bit *= 2
        return out

    barrier = pltpu.get_barrier_semaphore()
    for k in range(1, n_code):
        pl.semaphore_signal(barrier, inc=1, device_id=(d, flip(o, k)), device_id_type=MESH)
    for j in range(1, n_y):
        pl.semaphore_signal(
            barrier, inc=1, device_id=((y + j) % n_y * 2 + core, o), device_id_type=MESH
        )
    pl.semaphore_signal(barrier, inc=1, device_id=(mate, o), device_id_type=MESH)

    book = unnorm.at[n_code - 1]
    load = pltpu.make_async_copy(book_hbm, book.at[pl.ds(0, own_blocks)], book_sem)
    load.start()
    asked[0] = want_ref[o]
    own = pltpu.make_async_copy(want_ref.at[o], ids.at[0], smem_sem.at[0])
    own.start()
    pl.semaphore_wait(barrier, n_code - 1 + n_y - 1 + 1)

    asks = []
    for k in range(1, n_code):
        peer = flip(o, k)
        copy = remote(want_ref.at[peer], asked.at[k], id_send.at[k], id_recv.at[k], d, peer)
        copy.start()
        asks.append(copy)

    def gate(kb, c):
        count = counts_ref[kb]
        for k in range(n_code):
            slot = turn(k)
            hit = jnp.float32(1e30)
            for l in range(LIST_MAX):
                same = (slots_ref[kb, l] == slot) & (count > l)
                hit = jnp.where(same, jnp.float32(0.0), hit)
            less[kb, k] = hit
        return c

    def serve_copy(k):
        peer = flip(o, k)
        return remote(served.at[k], fetched.at[k], f_send.at[k], f_recv.at[k], d, peer)

    def move(k):
        return pltpu.make_async_copy(asked.at[k], ids.at[k], smem_sem.at[k])

    load.wait()
    own.wait()
    first = unnorm[n_code - 1, ids[0, 0, 0]]
    served[0] = first
    fetched[0] = first
    serves = []
    for k in range(1, n_code + 1):
        if k < n_code:
            asks[k - 1].wait_recv()
            move(k).start()
        if k > 1:
            move(k - 1).wait()
            served[k - 1] = unnorm[n_code - 1, ids[k - 1, 0, 0]]
            copy = serve_copy(k - 1)
            copy.start()
            serves.append(copy)

    kext[:, 128:256] = jnp.ones((keys, 128), jnp.bfloat16)
    kext[:, 0:128] = keys_ref[...]

    def turn_keys(c, carry):
        at = pl.ds(pl.multiple_of(c * block, block), block)
        turned = jnp.transpose(keys_ref[at, :])
        kst[0:128, at] = turned
        kst[128:256, at] = turned
        return carry

    lax.fori_loop(0, key_blocks, turn_keys, 0)
    lax.fori_loop(0, key_blocks, gate, 0)

    def score(k, blocks):
        value = blocks[k]
        scaled = value * scale
        hi = scaled.astype(jnp.bfloat16)
        words[:, 0:128] = hi
        words[:, 128:256] = (scaled - hi.astype(jnp.float32)).astype(jnp.bfloat16)
        half = (0.5 * scale) * jnp.sum(value * value, axis=1, keepdims=True)
        norms[...] = jnp.broadcast_to(half, (CBLK, 128))

        def some(i, c):
            for u in range(8):
                q = i * 8 + u
                cols = pl.ds(pl.multiple_of(q * 256, 256), 256)
                right = kst[:, cols]
                for h in range(2):
                    rows = slice(h * 128, (h + 1) * 128)
                    raw = jnp.dot(words[rows, :], right, preferred_element_type=jnp.float32)
                    s = raw - jnp.tile(norms[rows, :], (1, 2))
                    s = s.reshape(16, 8, 256)
                    top = jnp.max(s, axis=0)
                    e = jnp.exp2(s - top[None])
                    peaks[k, h, :, cols] = top
                    totals[k, h, :, cols] = jnp.sum(e, axis=0)
                    e = e.reshape(128, 256)
                    unnorm[k, 2 * q, rows, :] = e[:, 0:128]
                    unnorm[k, 2 * q + 1, rows, :] = e[:, 128:256]
            return c

        lax.fori_loop(0, keys // 256 // 8, some, 0)

    def normalise(last):
        def one(kb, c):
            cols = pl.ds(pl.multiple_of(kb * block, block), block)
            top = jnp.full((8, block), -3e38, jnp.float32)
            for k in range(n_code):
                for h in range(2):
                    top = jnp.maximum(top, peaks[k, h, :, cols] - less[kb, k])
            peak = jnp.max(top, axis=0, keepdims=True)
            total = jnp.zeros((8, block), jnp.float32)
            for k in range(n_code):
                for h in range(2):
                    w = jnp.exp2((peaks[k, h, :, cols] - less[kb, k]) - peak)
                    total = total + w * totals[k, h, :, cols]
                    peaks[k, h, :, cols] = w
            total = jnp.sum(total, axis=0, keepdims=True)
            if last:
                logsum_ref[kb] = peak * math.log(2.0) + jnp.log(total)
            inv = 1.0 / total
            for k in range(n_code):
                for h in range(2):
                    peaks[k, h, :, cols] = peaks[k, h, :, cols] * inv
            return c

        lax.fori_loop(0, key_blocks, one, 0)

    def collect(k):
        total = None
        for q in range(keys // 512):
            halves = []
            for h in range(2):
                rows = slice(h * 128, (h + 1) * 128)
                tiles = []
                for u in range(4):
                    e = unnorm[k, q * 4 + u, rows, :].reshape(16, 8, 128)
                    w = peaks[k, h, :, pl.ds((q * 4 + u) * 128, 128)]
                    tiles.append((e * w[None]).reshape(128, 128).astype(jnp.bfloat16))
                halves.append(jnp.concatenate(tiles, axis=1))
            piece = jnp.dot(
                jnp.concatenate(halves, axis=0), kext[q * 512 : (q + 1) * 512, :],
                preferred_element_type=jnp.float32,
            )
            total = piece if total is None else total + piece
        part[...] = total
        for h in range(2):
            turned = jnp.transpose(part[h * 128 : (h + 1) * 128, 128:256])
            sums[k, CBLK + h : CBLK + h + 1, :] = turned[0:1, :]
        sums[k, CBLK + 2 :, :] = want_ref[turn(k), 2:, :].astype(jnp.float32)
        sums[k, :CBLK, :] = part[:, 0:128]

    def held(k, j):
        return ((y + n_y - j) % n_y * 2 + core) * n_code + turn(k)

    order = list(range(1, n_code)) + [0]
    backs = []
    wide = list(range(far, n_code))
    close = list(range(2, far))
    beside = list(range(1, min(2, far)))
    beside = list(range(1, min(2, far)))
    inner = wide[:1] + close + wide[1:2] + [0] + beside + wide[2:]
    outer = close + [0] + wide[:1] + beside + wide[1:]
    inner_in = close + wide[:2] + beside + wide[2:]
    outer_in = beside + wide[:1] + wide[2:] + close[:1] + wide[1:2] + close[1:]
    middle = (o // far % 2) != (o // max(far // 2, 1) % 2)

    def choose(i, first, second):
        return jnp.where(middle, first[i], second[i])

    def pick(p):
        out = choose(0, inner, outer)
        for i in range(1, n_code):
            out = jnp.where(p == i, choose(i, inner, outer), out)
        return out

    waits = [("y", i) for i in range(n_code)]
    events = [("a", i) for i in range(min(far, n_code - 1))]
    for i in range(len(events), n_code - 1):
        take = 2 if i < n_code - 2 else 1
        events += waits[:take] + [("a", i)]
        waits = waits[take:]
    events += waits

    for sweep in range(sweeps):
        reply = sweep + 1 < sweeps
        con_ref = con_refs[sweep]
        blocks = fetched if sweep == 0 else back

        def scoring(k, c):
            @pl.when(k > 0)
            def _():
                if sweep == 0:
                    serve_copy_at(k).wait_recv()
                else:
                    back_copy_at(k).wait_recv()

            score(k, blocks)
            return c

        def serve_copy_at(k):
            return remote(served.at[k], fetched.at[k], f_send.at[k], f_recv.at[k], d, turn(k))

        def back_copy_at(k):
            return remote(stage.at[k], back.at[k], b_send.at[k], b_recv.at[k], d, turn(k))

        lax.fori_loop(0, n_code, scoring, 0)
        normalise(not reply)

        def across(k):
            return remote(
                sums.at[k], con_ref.at[d * n_code + o],
                a_send.at[sweep, k], a_recv.at[sweep, k], d, turn(k),
            )

        def to_y(k, j):
            row = held(k, 0)
            return remote(
                con_ref.at[row], con_ref.at[row],
                y_send.at[sweep, j, k], y_recv.at[sweep, j, k],
                (y + j) % n_y * 2 + core, o,
            )

        def own_y(j):
            return remote(
                sums.at[0], con_ref.at[d * n_code + o],
                y_send.at[sweep, j, 0], y_recv.at[sweep, j, 0],
                (y + j) % n_y * 2 + core, o,
            )

        def own_mate():
            return remote(
                sums.at[0], con_ref.at[d * n_code + o],
                c_send.at[sweep, 0, 0], c_recv.at[sweep, 0, 0], mate, o,
            )

        def to_mate(k, j):
            row = held(k, j)
            return remote(
                con_ref.at[row], con_ref.at[row],
                c_send.at[sweep, j, k], c_recv.at[sweep, j, k], mate, o,
            )

        if reply:
            acc[...] = jnp.zeros_like(acc)

        def absorb(row):
            if not reply:
                return
            here = con_ref[row, pl.ds(CBLK + 2, 1), :]

            def one(i, c):
                same = (asked[i, pl.ds(0, 1), :].astype(jnp.float32) == here).astype(jnp.float32)
                acc[i] += con_ref[row] * same
                return c

            lax.fori_loop(0, n_code, one, 0)

        mine = pltpu.make_async_copy(sums.at[0], con_ref.at[d * n_code + o], own_sem)

        def depart(k):
            @pl.when(k > 0)
            def _():
                across(k).start()

            @pl.when(k == 0)
            def _():
                mine.start()
                for j in range(1, n_y):
                    own_y(j).start()
                own_mate().start()

        def produce(p, c):
            collect(pick(p))

            @pl.when(p > 0)
            def _():
                depart(pick(p - 1))

            return c

        lax.fori_loop(0, n_code, produce, 0)
        mine.wait()
        depart(pick(n_code - 1))
        absorb(held(0, 0))
        for kind, i in events:
            if kind == "a":
                k = choose(i, inner_in, outer_in)
                across(k).wait_recv()
                for j in range(1, n_y):
                    to_y(k, j).start()
                to_mate(k, 0).start()
                absorb(held(k, 0))
            else:
                k = choose(i - 1, inner_in, outer_in) if i else 0
                for j in range(1, n_y):
                    to_y(k, j).wait_recv()
                    to_mate(k, j).start()
                    absorb(held(k, j))
                to_mate(k, 0).wait_recv()
                absorb(held(k, 0) + (1 - 2 * core) * n_code)
        for i in range(n_code):
            k = choose(i - 1, inner_in, outer_in) if i else 0
            for j in range(1, n_y):
                to_mate(k, j).wait_recv()
                absorb(held(k, j) + (1 - 2 * core) * n_code)
        for k in range(1, n_code):
            across(k).wait_send()
        for k in range(n_code):
            for j in range(1, n_y):
                to_y(k, j).wait_send()
                to_mate(k, j).wait_send()
            to_mate(k, 0).wait_send()
        if reply:
            for at, k in enumerate(order):
                for h in range(2):
                    inv = 1.0 / (acc[k, pl.ds(CBLK + h, 1), :] + 1.0)
                    column = jnp.transpose(jnp.broadcast_to(inv, (128, 128)))
                    rows = pl.ds(h * 128, 128)
                    fresh = (acc[k, rows, :] + served[k, rows, :]) * column
                    if k == 0:
                        back[0, rows, :] = fresh
                    else:
                        stage[k, rows, :] = fresh
                if at > 0:
                    copy = back_copy_at(order[at - 1])
                    copy.start()
                    backs.append(copy)
    for copy in asks + serves + backs:
        copy.wait_send()


def finish_kernel(n, own_blocks, sweeps, *refs):
    con_hbm = refs[:sweeps]
    book_hbm, out_hbm = refs[sweeps : sweeps + 2]
    con, total, mass, ids, con_sem, book_sem, out_sem = refs[sweeps + 2 :]
    book = pltpu.make_async_copy(book_hbm, total, book_sem)
    book.start()
    half = n // 2

    def load(t, h):
        rows = pl.ds(h * half, half)
        return pltpu.make_async_copy(con_hbm[t].at[rows], con.at[rows], con_sem.at[h])

    load(0, 0).start()
    load(0, 1).start()
    outs = []
    for t in range(sweeps):
        mass[...] = jnp.ones_like(mass)
        for h in range(2):
            load(t, h).wait()
            if t == 0:

                def name(j, c):
                    for u in range(4):
                        i = j * 4 + u
                        ids[i] = jnp.max(con[i, pl.ds(CBLK + 2, 1), :]).astype(jnp.int32)
                    return c

                lax.fori_loop(h * half // 4, (h + 1) * half // 4, name, 0)
                if h == 0:
                    book.wait()

            def add(j, c):
                b = ids[j]
                total[b] += con[j, :CBLK, :]
                for g in range(2):
                    row = pl.ds(g * (mass.shape[0] // 2) + b, 1)
                    mass[row, :] += con[j, pl.ds(CBLK + g, 1), :]
                return c

            lax.fori_loop(h * half, (h + 1) * half, add, 0)
            if t + 1 < sweeps:
                load(t + 1, h).start()
        columns = jnp.transpose(1.0 / mass[...])
        for b in range(own_blocks):
            for g in range(2):
                lane = g * (mass.shape[0] // 2) + b
                total[b, g * 128 : (g + 1) * 128, :] = (
                    total[b, g * 128 : (g + 1) * 128, :] * columns[:, lane : lane + 1]
                )
            if t + 1 == sweeps:
                out = pltpu.make_async_copy(total.at[b], out_hbm.at[b], out_sem.at[b])
                out.start()
                outs.append(out)
    for out in outs:
        out.wait()


def assign_kernel(
    n_slots, key_blocks, block, feature,
    slots_ref, counts_ref, fetched_ref, keys_ref, want_ref,
    sums_ref, logsum_ref,
    words, norms, kst, kext, picked, scores, post, acc,
):
    scale = math.log2(math.e) / math.sqrt(feature)

    for s in range(n_slots):
        value = fetched_ref[s]
        scaled = value * scale
        hi = scaled.astype(jnp.bfloat16)
        words[s, :, 0:128] = hi
        words[s, :, 128:256] = (scaled - hi.astype(jnp.float32)).astype(jnp.bfloat16)
        half = (0.5 * scale) * jnp.sum(value * value, axis=1, keepdims=True)
        norms[s] = jnp.broadcast_to(half, (CBLK, 128))
        acc[s] = jnp.zeros((CBLK, 256), jnp.float32)
    kext[:, 128:256] = jnp.ones((block, 128), jnp.bfloat16)

    def key_block(kb, c):
        keys = keys_ref[pl.ds(pl.multiple_of(kb * block, block), block), :]
        kext[:, 0:128] = keys
        turned = jnp.transpose(keys)
        kst[0:128, :] = turned
        kst[128:256, :] = turned
        count = counts_ref[kb]
        slots = [slots_ref[kb, l] for l in range(LIST_MAX)]
        for l in range(LIST_MAX):
            picked[l * CBLK : (l + 1) * CBLK, :] = words[slots[l]]
        raw = jnp.dot(picked[...], kst[...], preferred_element_type=jnp.float32)
        top = jnp.full((8, block), -3e38, jnp.float32)
        for l in range(LIST_MAX):
            rows = slice(l * CBLK, (l + 1) * CBLK)
            less = norms[slots[l]] + jnp.where(l < count, 0.0, 1e30)
            s = raw[rows] - jnp.tile(less, (1, block // 128))
            scores[rows, :] = s
            top = jnp.maximum(top, jnp.max(s.reshape(CBLK // 8, 8, block), axis=0))
        peak = jnp.max(top, axis=0, keepdims=True)
        total = jnp.zeros((8, block), jnp.float32)
        for l in range(LIST_MAX):
            rows = slice(l * CBLK, (l + 1) * CBLK)
            e = jnp.exp2(scores[rows, :] - peak)
            scores[rows, :] = e
            total = total + jnp.sum(e.reshape(CBLK // 8, 8, block), axis=0)
        total = jnp.sum(total, axis=0, keepdims=True)
        logsum_ref[kb] = peak * math.log(2.0) + jnp.log(total)
        inv = 1.0 / total
        post[...] = (scores[...] * inv).astype(jnp.bfloat16)
        weighted = jnp.dot(post[...], kext[...], preferred_element_type=jnp.float32)
        for l in range(LIST_MAX):
            acc[slots[l]] += weighted[l * CBLK : (l + 1) * CBLK]
        return c

    lax.fori_loop(0, key_blocks, key_block, 0)

    for s in range(n_slots):
        sums_ref[s, :CBLK, :] = acc[s, :, 0:128]
        for h in range(2):
            turned = jnp.transpose(acc[s, h * 128 : (h + 1) * 128, 128:256])
            sums_ref[s, CBLK + h : CBLK + h + 1, :] = turned[0:1, :]
        sums_ref[s, CBLK + 2 :, :] = want_ref[s, 2:, :].astype(jnp.float32)


def on_device(cached_keys, codebook, block_lists, counts):
    n_dp = lax.axis_size("dp")
    n_code = lax.axis_size("code")
    n = n_dp * n_code
    own_rows, feature = codebook.shape
    own_blocks = own_rows // CBLK
    key_blocks = block_lists.shape[0]
    block = cached_keys.shape[0] // key_blocks
    f32 = jnp.float32
    dma = pltpu.SemaphoreType.DMA

    slots = block_lists // own_blocks
    local = block_lists % own_blocks
    wanted = jnp.max(
        jnp.where(
            slots.reshape(-1)[:, None] == jnp.arange(128)[None, :], local.reshape(-1)[:, None], 0
        ),
        axis=0,
    )
    want = jnp.broadcast_to(wanted[:n_code, None, None], (n_code, 8, 128)).astype(jnp.int32)
    blocks = jax.ShapeDtypeStruct((n_code, CBLK, feature), f32)
    sums_shape = jax.ShapeDtypeStruct((n_code, CBLK + MROWS, feature), f32)
    con_shape = jax.ShapeDtypeStruct((n, CBLK + MROWS, feature), f32)
    n_y = n_dp // 2

    def params(**kw):
        return pltpu.CompilerParams(vmem_limit_bytes=VLIMIT, **kw)

    book = codebook.reshape(own_blocks, CBLK, feature)

    def finish(parts, held):
        return pl.pallas_call(
            functools.partial(finish_kernel, n, own_blocks, len(parts)),
            out_shape=jax.ShapeDtypeStruct((own_blocks, CBLK, feature), f32),
            in_specs=[ANY] * (len(parts) + 1),
            out_specs=ANY,
            scratch_shapes=[
                pltpu.VMEM(con_shape.shape, f32),
                pltpu.VMEM((own_blocks, CBLK, feature), f32),
                pltpu.VMEM((max(128, 2 * own_blocks), 128), f32),
                pltpu.SMEM((n,), jnp.int32),
                dma((2,)), dma, dma((own_blocks,)),
            ],
            compiler_params=params(),
        )(*parts, held)

    keys = key_blocks * block
    joint = (
        ITERS * n * (CBLK + MROWS) * feature * 4 <= HELD_BYTES
        and own_blocks * 128 <= keys
        and n_code * CBLK * keys * 4 <= HELD_BYTES * 2 + HELD_BYTES // 2
        and keys % 2048 == 0 and block % 512 == 0
    )
    if joint:
        bf16 = jnp.bfloat16
        results = pl.pallas_call(
            functools.partial(
                sweeps_kernel, n_dp, n_code, key_blocks, block, own_blocks, feature, ITERS
            ),
            out_shape=(con_shape,) * ITERS
            + (jax.ShapeDtypeStruct((key_blocks, 1, block), f32),),
            in_specs=[SM, SM, VM, VM, ANY],
            out_specs=(VM,) * (ITERS + 1),
            scratch_shapes=[
                pltpu.VMEM((n_code, keys // 128, CBLK, 128), f32),
                pltpu.VMEM((n_code, 2, 8, keys), f32),
                pltpu.VMEM((n_code, 2, 8, keys), f32),
                pltpu.VMEM((CBLK, 256), bf16),
                pltpu.VMEM((CBLK, 128), f32),
                pltpu.VMEM((256, keys), bf16),
                pltpu.VMEM((keys, 256), bf16),
                pltpu.VMEM(sums_shape.shape, f32),
                pltpu.VMEM(sums_shape.shape, f32),
                pltpu.VMEM(blocks.shape, f32),
                pltpu.VMEM(blocks.shape, f32),
                pltpu.VMEM(blocks.shape, f32),
                pltpu.VMEM(blocks.shape, f32),
                pltpu.VMEM((n_code, 8, 128), jnp.int32),
                pltpu.VMEM((CBLK, 256), f32),
                pltpu.SMEM((key_blocks, n_code), f32),
                pltpu.SMEM((n_code, 8, 128), jnp.int32),
                dma((n_code,)), dma((n_code,)),
                dma((n_code,)), dma((n_code,)),
                dma((n_code,)), dma((n_code,)),
                dma((ITERS, n_code)), dma((ITERS, n_code)),
                dma((ITERS, n_y, n_code)), dma((ITERS, n_y, n_code)),
                dma((ITERS, n_y, n_code)), dma((ITERS, n_y, n_code)),
                dma, dma, dma((n_code,)),
            ],
            compiler_params=params(collective_id=0, has_side_effects=True),
        )(slots, counts, want, cached_keys, book)
        current = finish(results[:ITERS], book)
        return (current.reshape(own_rows, feature), results[ITERS].reshape(-1))

    fetched, served, asked = pl.pallas_call(
        functools.partial(fetch_kernel, n_code),
        out_shape=(blocks, blocks, jax.ShapeDtypeStruct((n_code, 8, 128), jnp.int32)),
        in_specs=[VM, ANY],
        out_specs=(VM, VM, VM),
        scratch_shapes=[
            pltpu.VMEM((own_blocks, CBLK, feature), f32),
            pltpu.SMEM((n_code, 8, 128), jnp.int32),
            dma((n_code,)), dma((n_code,)), dma((n_code,)), dma((n_code,)),
            dma, dma, dma((n_code,)),
        ],
        compiler_params=params(collective_id=0, has_side_effects=True),
    )(want, book)
    current = book
    for sweep in range(ITERS):
        reply = sweep + 1 < ITERS
        sems = [
            dma((n_code,)), dma((n_code,)),
            dma((n_y, n_code)), dma((n_y, n_code)),
            dma((n_y, n_code)), dma((n_y, n_code)),
            dma,
        ]
        sums, logsum = pl.pallas_call(
            functools.partial(assign_kernel, n_code, key_blocks, block, feature),
            out_shape=(sums_shape, jax.ShapeDtypeStruct((key_blocks, 1, block), f32)),
            in_specs=[SM, SM, VM, VM, VM],
            out_specs=(VM, VM),
            scratch_shapes=[
                pltpu.VMEM((n_code, CBLK, 256), jnp.bfloat16),
                pltpu.VMEM((n_code, CBLK, 128), f32),
                pltpu.VMEM((256, block), jnp.bfloat16),
                pltpu.VMEM((block, 256), jnp.bfloat16),
                pltpu.VMEM((LIST_MAX * CBLK, 256), jnp.bfloat16),
                pltpu.VMEM((LIST_MAX * CBLK, block), f32),
                pltpu.VMEM((LIST_MAX * CBLK, block), jnp.bfloat16),
                pltpu.VMEM((n_code, CBLK, 256), f32),
            ],
            compiler_params=params(),
        )(slots, counts, fetched, cached_keys, want)
        if reply:
            con, fetched = pl.pallas_call(
                functools.partial(exchange_kernel, n_dp, n_code, True),
                out_shape=(con_shape, blocks),
                in_specs=[VM, VM, VM],
                out_specs=(VM, VM),
                scratch_shapes=[
                    pltpu.VMEM(sums_shape.shape, f32), pltpu.VMEM(blocks.shape, f32)
                ] + sems + [dma((n_code,)), dma((n_code,))],
                compiler_params=params(collective_id=1 + sweep, has_side_effects=True),
            )(sums, served, asked)
        else:
            con = pl.pallas_call(
                functools.partial(exchange_kernel, n_dp, n_code, False),
                out_shape=con_shape,
                in_specs=[VM],
                out_specs=VM,
                scratch_shapes=sems,
                compiler_params=params(collective_id=1 + sweep, has_side_effects=True),
            )(sums)
        current = finish([con], current)
        if reply:
            current, fetched = lax.optimization_barrier((current, fetched))
    return (current.reshape(own_rows, feature), logsum.reshape(-1))


def solution(mesh):
    in_specs = (
        P(("dp", "code"), None),
        P("code", None),
        P(("dp", "code"), None),
        P(("dp", "code")),
    )
    out_specs = (P("code", None), P(("dp", "code")))
    return jax.shard_map(
        on_device, mesh=mesh, in_specs=in_specs, out_specs=out_specs, check_vma=False
    )
```

```python
import functools
import math

import jax
import jax.numpy as jnp
from jax import lax
from jax.experimental import pallas as pl
from jax.experimental.pallas import tpu as pltpu
from jax.sharding import PartitionSpec as P

CBLK = 256
LIST_MAX = 6
ITERS = 2
MROWS = 8
MESH = pl.DeviceIdType.MESH
VLIMIT = 60 * 1024 * 1024
HELD_BYTES = 16 * 1024 * 1024

VM = pl.BlockSpec(memory_space=pltpu.VMEM)
SM = pl.BlockSpec(memory_space=pltpu.SMEM)
ANY = pl.BlockSpec(memory_space=pl.ANY)


def flip(value, bits):
    out = value
    bit = 1
    while bit <= bits:
        if bits & bit:
            out = out + bit * (1 - 2 * (value // bit % 2))
        bit *= 2
    return out


def remote(src, dst, send, recv, dp, code):
    return pltpu.make_async_remote_copy(
        src_ref=src, dst_ref=dst, send_sem=send, recv_sem=recv,
        device_id=(dp, code), device_id_type=MESH,
    )


def fetch_kernel(
    n_code, want_ref, book_hbm, out_ref, served_ref, asked_ref,
    book, ids, id_send, id_recv, send_sem, recv_sem, book_sem, own_sem, smem_sem,
):
    d = lax.axis_index("dp")
    o = lax.axis_index("code")
    barrier = pltpu.get_barrier_semaphore()
    for k in range(1, n_code):
        pl.semaphore_signal(barrier, inc=1, device_id=(d, flip(o, k)), device_id_type=MESH)
    load = pltpu.make_async_copy(book_hbm, book, book_sem)
    load.start()
    own = pltpu.make_async_copy(want_ref.at[o], asked_ref.at[o], own_sem)
    own.start()
    pl.semaphore_wait(barrier, n_code - 1)
    asks = []
    for k in range(1, n_code):
        peer = flip(o, k)
        copy = remote(
            want_ref.at[peer], asked_ref.at[o], id_send.at[k], id_recv.at[k], d, peer
        )
        copy.start()
        asks.append(copy)
    load.wait()
    copies = []
    for k in range(1, n_code):
        peer = flip(o, k)
        asks[k - 1].wait_recv()
        move = pltpu.make_async_copy(asked_ref.at[peer], ids.at[k], smem_sem.at[k])
        move.start()
        move.wait()
        served_ref[peer] = book[ids[k, 0, 0]]
        copy = remote(
            served_ref.at[peer], out_ref.at[o], send_sem.at[k], recv_sem.at[k], d, peer
        )
        copy.start()
        copies.append(copy)
    own.wait()
    move = pltpu.make_async_copy(asked_ref.at[o], ids.at[0], smem_sem.at[0])
    move.start()
    move.wait()
    block = book[ids[0, 0, 0]]
    served_ref[o] = block
    out_ref[o] = block
    for ask in asks:
        ask.wait_send()
    for copy in copies:
        copy.wait()


def exchange_kernel(n_dp, n_code, reply, *refs):
    if reply:
        (sums_ref, served_ref, asked_ref, con_ref, back_ref, acc, stage,
         a_send, a_recv, y_send, y_recv, c_send, c_recv, own_sem, b_send, b_recv) = refs
    else:
        (sums_ref, con_ref,
         a_send, a_recv, y_send, y_recv, c_send, c_recv, own_sem) = refs
    d = lax.axis_index("dp")
    o = lax.axis_index("code")
    n_y = n_dp // 2
    y = d // 2
    core = d % 2
    mate = y * 2 + 1 - core
    barrier = pltpu.get_barrier_semaphore()
    for k in range(1, n_code):
        pl.semaphore_signal(barrier, inc=1, device_id=(d, flip(o, k)), device_id_type=MESH)
    for j in range(1, n_y):
        pl.semaphore_signal(
            barrier, inc=1, device_id=((y + j) % n_y * 2 + core, o), device_id_type=MESH
        )
    pl.semaphore_signal(barrier, inc=1, device_id=(mate, o), device_id_type=MESH)
    own = pltpu.make_async_copy(sums_ref.at[o], con_ref.at[d * n_code + o], own_sem)
    own.start()
    pl.semaphore_wait(barrier, n_code - 1 + n_y - 1 + 1)

    sends = []
    across = []
    for k in range(1, n_code):
        peer = flip(o, k)
        copy = remote(
            sums_ref.at[peer], con_ref.at[d * n_code + o], a_send.at[k], a_recv.at[k], d, peer
        )
        copy.start()
        across.append(copy)
        sends.append(copy)

    def to_y(k, j):
        row = d * n_code + flip(o, k)
        return remote(
            con_ref.at[row], con_ref.at[row], y_send.at[j, k], y_recv.at[j, k],
            (y + j) % n_y * 2 + core, o,
        )

    def held(k, j):
        return ((y + n_y - j) % n_y * 2 + core) * n_code + flip(o, k)

    def to_mate(k, j):
        row = held(k, j)
        return remote(
            con_ref.at[row], con_ref.at[row], c_send.at[j, k], c_recv.at[j, k], mate, o
        )

    if reply:
        acc[...] = jnp.zeros_like(acc)

    def absorb(row):
        if not reply:
            return
        here = con_ref[row, pl.ds(CBLK + 2, 1), :]

        def one(i, c):
            same = (asked_ref[i, pl.ds(0, 1), :].astype(jnp.float32) == here).astype(jnp.float32)
            acc[i] += con_ref[row] * same
            return c

        lax.fori_loop(0, n_code, one, 0)

    y_copies = {}
    mates = {}
    for k in range(n_code):
        if k == 0:
            own.wait()
        else:
            across[k - 1].wait_recv()
        for j in range(1, n_y):
            copy = to_y(k, j)
            copy.start()
            y_copies[j, k] = copy
            sends.append(copy)
        copy = to_mate(k, 0)
        copy.start()
        mates[0, k] = copy
        sends.append(copy)
        absorb(held(k, 0))
    for k in range(n_code):
        for j in range(1, n_y):
            y_copies[j, k].wait_recv()
            copy = to_mate(k, j)
            copy.start()
            mates[j, k] = copy
            sends.append(copy)
            absorb(held(k, j))
        mates[0, k].wait_recv()
        absorb(held(k, 0) + (1 - 2 * core) * n_code)
    for k in range(n_code):
        for j in range(1, n_y):
            mates[j, k].wait_recv()
            absorb(held(k, j) + (1 - 2 * core) * n_code)
    if reply:
        backs = []
        for k in range(n_code):
            peer = flip(o, k)
            for h in range(2):
                inv = 1.0 / (acc[peer, pl.ds(CBLK + h, 1), :] + 1.0)
                column = jnp.transpose(jnp.broadcast_to(inv, (128, 128)))
                rows = pl.ds(h * 128, 128)
                fresh = (acc[peer, rows, :] + served_ref[peer, rows, :]) * column
                if k == 0:
                    back_ref[o, rows, :] = fresh
                else:
                    stage[k, rows, :] = fresh
        for k in range(n_code - 1, 0, -1):
            copy = remote(
                stage.at[k], back_ref.at[o], b_send.at[k], b_recv.at[k], d, flip(o, k)
            )
            copy.start()
            backs.append(copy)
        for copy in backs:
            copy.wait()
    for copy in sends:
        copy.wait_send()


def sweeps_kernel(n_dp, n_code, key_blocks, block, own_blocks, feature, sweeps, *refs):
    slots_ref, counts_ref, want_ref, keys_ref, book_hbm = refs[:5]
    out_refs = refs[5 : 5 + sweeps]
    logsum_ref = refs[5 + sweeps]
    con_refs = refs[6 + sweeps : 6 + 2 * sweeps]
    (unnorm, peaks, run_top, run_total, words, norms, kst, kext, sums, acc, stage, served,
     fetched, back, asked, part, less, ids,
     id_send, id_recv, f_send, f_recv, b_send, b_recv,
     a_send, a_recv, y_send, y_recv, c_send, c_recv,
     book_sem, own_sem, smem_sem, out_sem, keep_sem) = refs[6 + 2 * sweeps :]
    scale = math.log2(math.e) / math.sqrt(feature)
    keys = key_blocks * block
    chunks = keys // 128
    d = lax.axis_index("dp")
    o = lax.axis_index("code")
    n_y = n_dp // 2
    y = d // 2
    core = d % 2
    mate = y * 2 + 1 - core
    far = n_code // 2

    def turn(k):
        out = o
        bit = 1
        while bit < n_code:
            out = out + bit * (k // bit % 2) * (1 - 2 * (o // bit % 2))
            bit *= 2
        return out

    barrier = pltpu.get_barrier_semaphore()
    for k in range(1, n_code):
        pl.semaphore_signal(barrier, inc=1, device_id=(d, flip(o, k)), device_id_type=MESH)
    for j in range(1, n_y):
        pl.semaphore_signal(
            barrier, inc=1, device_id=((y + j) % n_y * 2 + core, o), device_id_type=MESH
        )
    pl.semaphore_signal(barrier, inc=1, device_id=(mate, o), device_id_type=MESH)

    book = unnorm.at[n_code - 1]
    load = pltpu.make_async_copy(book_hbm, book.at[pl.ds(0, own_blocks)], book_sem)
    load.start()
    asked[0] = want_ref[o]
    own = pltpu.make_async_copy(want_ref.at[o], ids.at[0], smem_sem.at[0])
    own.start()
    pl.semaphore_wait(barrier, n_code - 1 + n_y - 1 + 1)

    asks = []
    for k in range(1, n_code):
        peer = flip(o, k)
        copy = remote(want_ref.at[peer], asked.at[k], id_send.at[k], id_recv.at[k], d, peer)
        copy.start()
        asks.append(copy)

    def gate(kb, c):
        count = counts_ref[kb]
        for k in range(n_code):
            slot = turn(k)
            hit = jnp.float32(1e30)
            for l in range(LIST_MAX):
                same = (slots_ref[kb, l] == slot) & (count > l)
                hit = jnp.where(same, jnp.float32(0.0), hit)
            less[kb, k] = hit
        return c

    def serve_copy(k):
        peer = flip(o, k)
        return remote(served.at[k], fetched.at[k], f_send.at[k], f_recv.at[k], d, peer)

    def move(k):
        return pltpu.make_async_copy(asked.at[k], ids.at[k], smem_sem.at[k])

    load.wait()
    own.wait()
    first = unnorm[n_code - 1, ids[0, 0, 0]]
    served[0] = first
    fetched[0] = first
    serves = []
    for k in range(1, n_code + 1):
        if k < n_code:
            asks[k - 1].wait_recv()
            move(k).start()
        if k > 1:
            move(k - 1).wait()
            served[k - 1] = unnorm[n_code - 1, ids[k - 1, 0, 0]]
            copy = serve_copy(k - 1)
            copy.start()
            serves.append(copy)

    kext[:, 128:256] = jnp.ones((keys, 128), jnp.bfloat16)
    kext[:, 0:128] = keys_ref[...]

    def turn_keys(c, carry):
        at = pl.ds(pl.multiple_of(c * block, block), block)
        turned = jnp.transpose(keys_ref[at, :])
        kst[0:128, at] = turned
        kst[128:256, at] = turned
        return carry

    lax.fori_loop(0, key_blocks, turn_keys, 0)
    lax.fori_loop(0, key_blocks, gate, 0)

    def score(k, blocks):
        value = blocks[k]
        scaled = value * scale
        hi = scaled.astype(jnp.bfloat16)
        words[:, 0:128] = hi
        words[:, 128:256] = (scaled - hi.astype(jnp.float32)).astype(jnp.bfloat16)
        half = (0.5 * scale) * jnp.sum(value * value, axis=1, keepdims=True)
        norms[...] = jnp.broadcast_to(half, (CBLK, 128))

        def some(i, c):
            for u in range(8):
                q = i * 8 + u
                cols = pl.ds(pl.multiple_of(q * 256, 256), 256)
                right = kst[:, cols]
                away = less[q * 256 // block, k]
                tops, parts = [], []
                for h in range(2):
                    rows = slice(h * 128, (h + 1) * 128)
                    raw = jnp.dot(words[rows, :], right, preferred_element_type=jnp.float32)
                    s = raw - jnp.tile(norms[rows, :], (1, 2))
                    s = s.reshape(16, 8, 256)
                    top = jnp.max(s, axis=0)
                    e = jnp.exp2(s - top[None])
                    peaks[k, h, :, cols] = top
                    tops.append(top - away)
                    parts.append(jnp.sum(e, axis=0))
                    e = e.reshape(128, 256)
                    unnorm[k, 2 * q, rows, :] = e[:, 0:128]
                    unnorm[k, 2 * q + 1, rows, :] = e[:, 128:256]
                old = run_top[:, cols]
                new = jnp.maximum(old, jnp.maximum(tops[0], tops[1]))
                run_top[:, cols] = new
                run_total[:, cols] = run_total[:, cols] * jnp.exp2(old - new) + (
                    parts[0] * jnp.exp2(tops[0] - new) + parts[1] * jnp.exp2(tops[1] - new)
                )
            return c

        lax.fori_loop(0, keys // 256 // 8, some, 0)

    def normalise(last):
        def one(kb, c):
            cols = pl.ds(pl.multiple_of(kb * block, block), block)
            top = run_top[:, cols]
            peak = jnp.max(top, axis=0, keepdims=True)
            total = jnp.sum(run_total[:, cols] * jnp.exp2(top - peak), axis=0, keepdims=True)
            if last:
                row = peak * math.log(2.0) + jnp.log(total)
                for i in range(block // 128):
                    at = pl.ds(kb * (block // 128) + i, 1)
                    logsum_ref[at, :] = row[:, i * 128 : (i + 1) * 128]
            run_top[:, cols] = jnp.broadcast_to(peak, (8, block))
            run_total[:, cols] = jnp.broadcast_to(1.0 / total, (8, block))
            return c

        lax.fori_loop(0, key_blocks, one, 0)

    def collect(k):
        total = None
        for q in range(keys // 512):
            halves = []
            for h in range(2):
                rows = slice(h * 128, (h + 1) * 128)
                tiles = []
                for u in range(4):
                    e = unnorm[k, q * 4 + u, rows, :].reshape(16, 8, 128)
                    cols = pl.ds((q * 4 + u) * 128, 128)
                    w = (peaks[k, h, :, cols] - less[q * 512 // block, k]) - run_top[:, cols]
                    w = jnp.exp2(w) * run_total[:, cols]
                    tiles.append((e * w[None]).reshape(128, 128).astype(jnp.bfloat16))
                halves.append(jnp.concatenate(tiles, axis=1))
            piece = jnp.dot(
                jnp.concatenate(halves, axis=0), kext[q * 512 : (q + 1) * 512, :],
                preferred_element_type=jnp.float32,
            )
            total = piece if total is None else total + piece
        part[...] = total
        for h in range(2):
            turned = jnp.transpose(part[h * 128 : (h + 1) * 128, 128:256])
            sums[k, CBLK + h : CBLK + h + 1, :] = turned[0:1, :]
        sums[k, CBLK + 2 :, :] = want_ref[turn(k), 2:, :].astype(jnp.float32)
        sums[k, :CBLK, :] = part[:, 0:128]

    def held(k, j):
        return ((y + n_y - j) % n_y * 2 + core) * n_code + turn(k)

    keeps = []
    wide = list(range(far, n_code))
    close = list(range(2, far))
    beside = list(range(1, min(2, far)))
    beside = list(range(1, min(2, far)))
    inner = wide[:1] + close + wide[1:2] + [0] + beside + wide[2:]
    outer = close + [0] + wide[:1] + beside + wide[1:]
    inner_in = close + wide[:2] + beside + wide[2:]
    outer_in = beside + wide[:1] + wide[2:] + close[:1] + wide[1:2] + close[1:]
    middle = (o // far % 2) != (o // max(far // 2, 1) % 2)

    def choose(i, first, second):
        return jnp.where(middle, first[i], second[i])

    def table(p, first, second):
        out = choose(0, first, second)
        for i in range(1, n_code):
            out = jnp.where(p == i, choose(i, first, second), out)
        return out

    def pick(p):
        return table(p, inner, outer)

    waits = [("y", i) for i in range(n_code)]
    events = [("a", i) for i in range(min(far, n_code - 1))]
    for i in range(len(events), n_code - 1):
        take = 2 if i < n_code - 2 else 1
        events += waits[:take] + [("a", i)]
        waits = waits[take:]
    events += waits

    def serve_copy_at(k):
        return remote(served.at[k], fetched.at[k], f_send.at[k], f_recv.at[k], d, turn(k))

    def back_copy_at(k):
        return remote(stage.at[k], back.at[k], b_send.at[k], b_recv.at[k], d, turn(k))

    for sweep in range(sweeps):
        reply = sweep + 1 < sweeps
        con_ref = con_refs[sweep]
        blocks = fetched if sweep == 0 else back

        run_top[...] = jnp.full((8, keys), -3e38, jnp.float32)
        run_total[...] = jnp.zeros((8, keys), jnp.float32)

        def scoring(k, c):
            @pl.when(k > 0)
            def _():
                if sweep == 0:
                    serve_copy_at(k).wait_recv()
                else:
                    back_copy_at(k).wait_recv()

            score(k, blocks)
            return c

        lax.fori_loop(0, n_code, scoring, 0)
        normalise(not reply)

        def across(k):
            return remote(
                sums.at[k], con_ref.at[d * n_code + o],
                a_send.at[sweep, k], a_recv.at[sweep, k], d, turn(k),
            )

        def to_y(k, j):
            row = held(k, 0)
            return remote(
                con_ref.at[row], con_ref.at[row],
                y_send.at[sweep, j, k], y_recv.at[sweep, j, k],
                (y + j) % n_y * 2 + core, o,
            )

        def own_y(j):
            return remote(
                sums.at[0], con_ref.at[d * n_code + o],
                y_send.at[sweep, j, 0], y_recv.at[sweep, j, 0],
                (y + j) % n_y * 2 + core, o,
            )

        def own_mate():
            return remote(
                sums.at[0], con_ref.at[d * n_code + o],
                c_send.at[sweep, 0, 0], c_recv.at[sweep, 0, 0], mate, o,
            )

        def to_mate(k, j):
            row = held(k, j)
            return remote(
                con_ref.at[row], con_ref.at[row],
                c_send.at[sweep, j, k], c_recv.at[sweep, j, k], mate, o,
            )

        if reply:
            acc[...] = jnp.zeros_like(acc)

        def absorb(row):
            if not reply:
                pltpu.make_async_copy(
                    con_ref.at[row], out_refs[sweep].at[row], out_sem.at[row]
                ).start()
                return
            here = con_ref[row, pl.ds(CBLK + 2, 1), :]

            def one(i, c):
                same = (asked[i, pl.ds(0, 1), :].astype(jnp.float32) == here).astype(jnp.float32)
                acc[i] += con_ref[row] * same
                return c

            lax.fori_loop(0, n_code, one, 0)

        mine = pltpu.make_async_copy(sums.at[0], con_ref.at[d * n_code + o], own_sem)

        def depart(k):
            @pl.when(k > 0)
            def _():
                across(k).start()

            @pl.when(k == 0)
            def _():
                mine.start()
                for j in range(1, n_y):
                    own_y(j).start()
                own_mate().start()

        def produce(p, c):
            collect(pick(p))

            @pl.when(p > 0)
            def _():
                depart(pick(p - 1))

            return c

        lax.fori_loop(0, n_code, produce, 0)
        mine.wait()
        depart(pick(n_code - 1))
        absorb(held(0, 0))
        for kind, i in events:
            if kind == "a":
                k = choose(i, inner_in, outer_in)
                across(k).wait_recv()
                for j in range(1, n_y):
                    to_y(k, j).start()
                to_mate(k, 0).start()
                absorb(held(k, 0))
            else:
                k = choose(i - 1, inner_in, outer_in) if i else 0
                for j in range(1, n_y):
                    to_y(k, j).wait_recv()
                    to_mate(k, j).start()
                    absorb(held(k, j))
                to_mate(k, 0).wait_recv()
                absorb(held(k, 0) + (1 - 2 * core) * n_code)
        for i in range(n_code):
            k = choose(i - 1, inner_in, outer_in) if i else 0
            for j in range(1, n_y):
                to_mate(k, j).wait_recv()
                absorb(held(k, j) + (1 - 2 * core) * n_code)
        for k in range(1, n_code):
            across(k).wait_send()
        for k in range(n_code):
            for j in range(1, n_y):
                to_y(k, j).wait_send()
                to_mate(k, j).wait_send()
            to_mate(k, 0).wait_send()
        if reply:
            for p in range(n_code):
                k = (p + 1) % n_code
                for h in range(2):
                    inv = 1.0 / (acc[k, pl.ds(CBLK + h, 1), :] + 1.0)
                    column = jnp.transpose(jnp.broadcast_to(inv, (128, 128)))
                    rows = pl.ds(h * 128, 128)
                    fresh = (acc[k, rows, :] + served[k, rows, :]) * column
                    if k == 0:
                        back[0, rows, :] = fresh
                    else:
                        stage[k, rows, :] = fresh
                if p > 0:
                    back_copy_at(p).start()
            keep = pltpu.make_async_copy(con_ref, out_refs[sweep], keep_sem.at[sweep])
            keep.start()
            keeps.append(keep)
    for row in range(n_dp * n_code):
        pltpu.make_async_copy(
            con_refs[-1].at[row], out_refs[-1].at[row], out_sem.at[row]
        ).wait()
    for k in range(1, n_code):
        back_copy_at(k).wait_send()
    for keep in keeps:
        keep.wait()
    for copy in asks + serves:
        copy.wait_send()


def finish_kernel(n, own_blocks, sweeps, *refs):
    con_hbm = refs[:sweeps]
    book_hbm, out_hbm = refs[sweeps : sweeps + 2]
    con, total, mass, ids, con_sem, book_sem, out_sem = refs[sweeps + 2 :]
    book = pltpu.make_async_copy(book_hbm, total, book_sem)
    book.start()
    half = n // 2

    def load(t, h):
        rows = pl.ds(h * half, half)
        return pltpu.make_async_copy(con_hbm[t].at[rows], con.at[rows], con_sem.at[h])

    load(0, 0).start()
    load(0, 1).start()
    outs = []
    for t in range(sweeps):
        mass[...] = jnp.ones_like(mass)
        for h in range(2):
            load(t, h).wait()
            if t == 0:

                def name(j, c):
                    for u in range(4):
                        i = j * 4 + u
                        ids[i] = jnp.max(con[i, pl.ds(CBLK + 2, 1), :]).astype(jnp.int32)
                    return c

                lax.fori_loop(h * half // 4, (h + 1) * half // 4, name, 0)
                if h == 0:
                    book.wait()

            def add(j, c):
                b = ids[j]
                total[b] += con[j, :CBLK, :]
                for g in range(2):
                    row = pl.ds(g * (mass.shape[0] // 2) + b, 1)
                    mass[row, :] += con[j, pl.ds(CBLK + g, 1), :]
                return c

            lax.fori_loop(h * half, (h + 1) * half, add, 0)
            if t + 1 < sweeps:
                load(t + 1, h).start()
        columns = jnp.transpose(1.0 / mass[...])
        for b in range(own_blocks):
            for g in range(2):
                lane = g * (mass.shape[0] // 2) + b
                total[b, g * 128 : (g + 1) * 128, :] = (
                    total[b, g * 128 : (g + 1) * 128, :] * columns[:, lane : lane + 1]
                )
            if t + 1 == sweeps:
                out = pltpu.make_async_copy(total.at[b], out_hbm.at[b], out_sem.at[b])
                out.start()
                outs.append(out)
    for out in outs:
        out.wait()


def assign_kernel(
    n_slots, key_blocks, block, feature,
    slots_ref, counts_ref, fetched_ref, keys_ref, want_ref,
    sums_ref, logsum_ref,
    words, norms, kst, kext, picked, scores, post, acc,
):
    scale = math.log2(math.e) / math.sqrt(feature)

    for s in range(n_slots):
        value = fetched_ref[s]
        scaled = value * scale
        hi = scaled.astype(jnp.bfloat16)
        words[s, :, 0:128] = hi
        words[s, :, 128:256] = (scaled - hi.astype(jnp.float32)).astype(jnp.bfloat16)
        half = (0.5 * scale) * jnp.sum(value * value, axis=1, keepdims=True)
        norms[s] = jnp.broadcast_to(half, (CBLK, 128))
        acc[s] = jnp.zeros((CBLK, 256), jnp.float32)
    kext[:, 128:256] = jnp.ones((block, 128), jnp.bfloat16)

    def key_block(kb, c):
        keys = keys_ref[pl.ds(pl.multiple_of(kb * block, block), block), :]
        kext[:, 0:128] = keys
        turned = jnp.transpose(keys)
        kst[0:128, :] = turned
        kst[128:256, :] = turned
        count = counts_ref[kb]
        slots = [slots_ref[kb, l] for l in range(LIST_MAX)]
        for l in range(LIST_MAX):
            picked[l * CBLK : (l + 1) * CBLK, :] = words[slots[l]]
        raw = jnp.dot(picked[...], kst[...], preferred_element_type=jnp.float32)
        top = jnp.full((8, block), -3e38, jnp.float32)
        for l in range(LIST_MAX):
            rows = slice(l * CBLK, (l + 1) * CBLK)
            less = norms[slots[l]] + jnp.where(l < count, 0.0, 1e30)
            s = raw[rows] - jnp.tile(less, (1, block // 128))
            scores[rows, :] = s
            top = jnp.maximum(top, jnp.max(s.reshape(CBLK // 8, 8, block), axis=0))
        peak = jnp.max(top, axis=0, keepdims=True)
        total = jnp.zeros((8, block), jnp.float32)
        for l in range(LIST_MAX):
            rows = slice(l * CBLK, (l + 1) * CBLK)
            e = jnp.exp2(scores[rows, :] - peak)
            scores[rows, :] = e
            total = total + jnp.sum(e.reshape(CBLK // 8, 8, block), axis=0)
        total = jnp.sum(total, axis=0, keepdims=True)
        logsum_ref[kb] = peak * math.log(2.0) + jnp.log(total)
        inv = 1.0 / total
        post[...] = (scores[...] * inv).astype(jnp.bfloat16)
        weighted = jnp.dot(post[...], kext[...], preferred_element_type=jnp.float32)
        for l in range(LIST_MAX):
            acc[slots[l]] += weighted[l * CBLK : (l + 1) * CBLK]
        return c

    lax.fori_loop(0, key_blocks, key_block, 0)

    for s in range(n_slots):
        sums_ref[s, :CBLK, :] = acc[s, :, 0:128]
        for h in range(2):
            turned = jnp.transpose(acc[s, h * 128 : (h + 1) * 128, 128:256])
            sums_ref[s, CBLK + h : CBLK + h + 1, :] = turned[0:1, :]
        sums_ref[s, CBLK + 2 :, :] = want_ref[s, 2:, :].astype(jnp.float32)


def on_device(cached_keys, codebook, block_lists, counts):
    n_dp = lax.axis_size("dp")
    n_code = lax.axis_size("code")
    n = n_dp * n_code
    own_rows, feature = codebook.shape
    own_blocks = own_rows // CBLK
    key_blocks = block_lists.shape[0]
    block = cached_keys.shape[0] // key_blocks
    f32 = jnp.float32
    dma = pltpu.SemaphoreType.DMA

    slots = block_lists // own_blocks
    local = block_lists % own_blocks
    wanted = jnp.max(
        jnp.where(
            slots.reshape(-1)[:, None] == jnp.arange(128)[None, :], local.reshape(-1)[:, None], 0
        ),
        axis=0,
    )
    want = jnp.broadcast_to(wanted[:n_code, None, None], (n_code, 8, 128)).astype(jnp.int32)
    blocks = jax.ShapeDtypeStruct((n_code, CBLK, feature), f32)
    sums_shape = jax.ShapeDtypeStruct((n_code, CBLK + MROWS, feature), f32)
    con_shape = jax.ShapeDtypeStruct((n, CBLK + MROWS, feature), f32)
    n_y = n_dp // 2

    def params(**kw):
        return pltpu.CompilerParams(vmem_limit_bytes=VLIMIT, **kw)

    book = codebook.reshape(own_blocks, CBLK, feature)

    def finish(parts, held):
        return pl.pallas_call(
            functools.partial(finish_kernel, n, own_blocks, len(parts)),
            out_shape=jax.ShapeDtypeStruct((own_blocks, CBLK, feature), f32),
            in_specs=[ANY] * (len(parts) + 1),
            out_specs=ANY,
            scratch_shapes=[
                pltpu.VMEM(con_shape.shape, f32),
                pltpu.VMEM((own_blocks, CBLK, feature), f32),
                pltpu.VMEM((max(128, 2 * own_blocks), 128), f32),
                pltpu.SMEM((n,), jnp.int32),
                dma((2,)), dma, dma((own_blocks,)),
            ],
            compiler_params=params(),
        )(*parts, held)

    keys = key_blocks * block
    joint = (
        ITERS * n * (CBLK + MROWS) * feature * 4 <= HELD_BYTES
        and own_blocks * 128 <= keys
        and n_code * CBLK * keys * 4 <= HELD_BYTES * 2 + HELD_BYTES // 2
        and keys % 2048 == 0 and block % 512 == 0
    )
    if joint:
        bf16 = jnp.bfloat16
        results = pl.pallas_call(
            functools.partial(
                sweeps_kernel, n_dp, n_code, key_blocks, block, own_blocks, feature, ITERS
            ),
            out_shape=(con_shape,) * ITERS
            + (jax.ShapeDtypeStruct((keys // 128, 128), f32),),
            in_specs=[SM, SM, VM, VM, ANY],
            out_specs=(ANY,) * ITERS + (VM,),
            scratch_shapes=[pltpu.VMEM(con_shape.shape, f32) for _ in range(ITERS)] + [
                pltpu.VMEM((n_code, keys // 128, CBLK, 128), f32),
                pltpu.VMEM((n_code, 2, 8, keys), f32),
                pltpu.VMEM((8, keys), f32),
                pltpu.VMEM((8, keys), f32),
                pltpu.VMEM((CBLK, 256), bf16),
                pltpu.VMEM((CBLK, 128), f32),
                pltpu.VMEM((256, keys), bf16),
                pltpu.VMEM((keys, 256), bf16),
                pltpu.VMEM(sums_shape.shape, f32),
                pltpu.VMEM(sums_shape.shape, f32),
                pltpu.VMEM(blocks.shape, f32),
                pltpu.VMEM(blocks.shape, f32),
                pltpu.VMEM(blocks.shape, f32),
                pltpu.VMEM(blocks.shape, f32),
                pltpu.VMEM((n_code, 8, 128), jnp.int32),
                pltpu.VMEM((CBLK, 256), f32),
                pltpu.SMEM((key_blocks, n_code), f32),
                pltpu.SMEM((n_code, 8, 128), jnp.int32),
                dma((n_code,)), dma((n_code,)),
                dma((n_code,)), dma((n_code,)),
                dma((n_code,)), dma((n_code,)),
                dma((ITERS, n_code)), dma((ITERS, n_code)),
                dma((ITERS, n_y, n_code)), dma((ITERS, n_y, n_code)),
                dma((ITERS, n_y, n_code)), dma((ITERS, n_y, n_code)),
                dma, dma, dma((n_code,)), dma((n,)), dma((ITERS,)),
            ],
            compiler_params=params(collective_id=0, has_side_effects=True),
        )(slots, counts, want, cached_keys, book)
        current = finish(results[:ITERS], book)
        return (current.reshape(own_rows, feature), results[ITERS].reshape(-1))

    fetched, served, asked = pl.pallas_call(
        functools.partial(fetch_kernel, n_code),
        out_shape=(blocks, blocks, jax.ShapeDtypeStruct((n_code, 8, 128), jnp.int32)),
        in_specs=[VM, ANY],
        out_specs=(VM, VM, VM),
        scratch_shapes=[
            pltpu.VMEM((own_blocks, CBLK, feature), f32),
            pltpu.SMEM((n_code, 8, 128), jnp.int32),
            dma((n_code,)), dma((n_code,)), dma((n_code,)), dma((n_code,)),
            dma, dma, dma((n_code,)),
        ],
        compiler_params=params(collective_id=0, has_side_effects=True),
    )(want, book)
    current = book
    for sweep in range(ITERS):
        reply = sweep + 1 < ITERS
        sems = [
            dma((n_code,)), dma((n_code,)),
            dma((n_y, n_code)), dma((n_y, n_code)),
            dma((n_y, n_code)), dma((n_y, n_code)),
            dma,
        ]
        sums, logsum = pl.pallas_call(
            functools.partial(assign_kernel, n_code, key_blocks, block, feature),
            out_shape=(sums_shape, jax.ShapeDtypeStruct((key_blocks, 1, block), f32)),
            in_specs=[SM, SM, VM, VM, VM],
            out_specs=(VM, VM),
            scratch_shapes=[
                pltpu.VMEM((n_code, CBLK, 256), jnp.bfloat16),
                pltpu.VMEM((n_code, CBLK, 128), f32),
                pltpu.VMEM((256, block), jnp.bfloat16),
                pltpu.VMEM((block, 256), jnp.bfloat16),
                pltpu.VMEM((LIST_MAX * CBLK, 256), jnp.bfloat16),
                pltpu.VMEM((LIST_MAX * CBLK, block), f32),
                pltpu.VMEM((LIST_MAX * CBLK, block), jnp.bfloat16),
                pltpu.VMEM((n_code, CBLK, 256), f32),
            ],
            compiler_params=params(),
        )(slots, counts, fetched, cached_keys, want)
        if reply:
            con, fetched = pl.pallas_call(
                functools.partial(exchange_kernel, n_dp, n_code, True),
                out_shape=(con_shape, blocks),
                in_specs=[VM, VM, VM],
                out_specs=(VM, VM),
                scratch_shapes=[
                    pltpu.VMEM(sums_shape.shape, f32), pltpu.VMEM(blocks.shape, f32)
                ] + sems + [dma((n_code,)), dma((n_code,))],
                compiler_params=params(collective_id=1 + sweep, has_side_effects=True),
            )(sums, served, asked)
        else:
            con = pl.pallas_call(
                functools.partial(exchange_kernel, n_dp, n_code, False),
                out_shape=con_shape,
                in_specs=[VM],
                out_specs=VM,
                scratch_shapes=sems,
                compiler_params=params(collective_id=1 + sweep, has_side_effects=True),
            )(sums)
        current = finish([con], current)
        if reply:
            current, fetched = lax.optimization_barrier((current, fetched))
    return (current.reshape(own_rows, feature), logsum.reshape(-1))


def solution(mesh):
    in_specs = (
        P(("dp", "code"), None),
        P("code", None),
        P(("dp", "code"), None),
        P(("dp", "code")),
    )
    out_specs = (P("code", None), P(("dp", "code")))
    return jax.shard_map(
        on_device, mesh=mesh, in_specs=in_specs, out_specs=out_specs, check_vma=False
    )
```

```python
import functools
import math

import jax
import jax.numpy as jnp
from jax import lax
from jax.experimental import pallas as pl
from jax.experimental.pallas import tpu as pltpu
from jax.sharding import PartitionSpec as P

CBLK = 256
LIST_MAX = 6
ITERS = 2
MROWS = 8
MESH = pl.DeviceIdType.MESH
VLIMIT = 60 * 1024 * 1024
HELD_BYTES = 16 * 1024 * 1024

VM = pl.BlockSpec(memory_space=pltpu.VMEM)
SM = pl.BlockSpec(memory_space=pltpu.SMEM)
ANY = pl.BlockSpec(memory_space=pl.ANY)


def flip(value, bits):
    out = value
    bit = 1
    while bit <= bits:
        if bits & bit:
            out = out + bit * (1 - 2 * (value // bit % 2))
        bit *= 2
    return out


def remote(src, dst, send, recv, dp, code):
    return pltpu.make_async_remote_copy(
        src_ref=src, dst_ref=dst, send_sem=send, recv_sem=recv,
        device_id=(dp, code), device_id_type=MESH,
    )


def fetch_kernel(
    n_code, want_ref, book_hbm, out_ref, served_ref, asked_ref,
    book, ids, id_send, id_recv, send_sem, recv_sem, book_sem, own_sem, smem_sem,
):
    d = lax.axis_index("dp")
    o = lax.axis_index("code")
    barrier = pltpu.get_barrier_semaphore()
    for k in range(1, n_code):
        pl.semaphore_signal(barrier, inc=1, device_id=(d, flip(o, k)), device_id_type=MESH)
    load = pltpu.make_async_copy(book_hbm, book, book_sem)
    load.start()
    own = pltpu.make_async_copy(want_ref.at[o], asked_ref.at[o], own_sem)
    own.start()
    pl.semaphore_wait(barrier, n_code - 1)
    asks = []
    for k in range(1, n_code):
        peer = flip(o, k)
        copy = remote(
            want_ref.at[peer], asked_ref.at[o], id_send.at[k], id_recv.at[k], d, peer
        )
        copy.start()
        asks.append(copy)
    load.wait()
    copies = []
    for k in range(1, n_code):
        peer = flip(o, k)
        asks[k - 1].wait_recv()
        move = pltpu.make_async_copy(asked_ref.at[peer], ids.at[k], smem_sem.at[k])
        move.start()
        move.wait()
        served_ref[peer] = book[ids[k, 0, 0]]
        copy = remote(
            served_ref.at[peer], out_ref.at[o], send_sem.at[k], recv_sem.at[k], d, peer
        )
        copy.start()
        copies.append(copy)
    own.wait()
    move = pltpu.make_async_copy(asked_ref.at[o], ids.at[0], smem_sem.at[0])
    move.start()
    move.wait()
    block = book[ids[0, 0, 0]]
    served_ref[o] = block
    out_ref[o] = block
    for ask in asks:
        ask.wait_send()
    for copy in copies:
        copy.wait()


def exchange_kernel(n_dp, n_code, reply, *refs):
    if reply:
        (sums_ref, served_ref, asked_ref, con_ref, back_ref, acc, stage,
         a_send, a_recv, y_send, y_recv, c_send, c_recv, own_sem, b_send, b_recv) = refs
    else:
        (sums_ref, con_ref,
         a_send, a_recv, y_send, y_recv, c_send, c_recv, own_sem) = refs
    d = lax.axis_index("dp")
    o = lax.axis_index("code")
    n_y = n_dp // 2
    y = d // 2
    core = d % 2
    mate = y * 2 + 1 - core
    barrier = pltpu.get_barrier_semaphore()
    for k in range(1, n_code):
        pl.semaphore_signal(barrier, inc=1, device_id=(d, flip(o, k)), device_id_type=MESH)
    for j in range(1, n_y):
        pl.semaphore_signal(
            barrier, inc=1, device_id=((y + j) % n_y * 2 + core, o), device_id_type=MESH
        )
    pl.semaphore_signal(barrier, inc=1, device_id=(mate, o), device_id_type=MESH)
    own = pltpu.make_async_copy(sums_ref.at[o], con_ref.at[d * n_code + o], own_sem)
    own.start()
    pl.semaphore_wait(barrier, n_code - 1 + n_y - 1 + 1)

    sends = []
    across = []
    for k in range(1, n_code):
        peer = flip(o, k)
        copy = remote(
            sums_ref.at[peer], con_ref.at[d * n_code + o], a_send.at[k], a_recv.at[k], d, peer
        )
        copy.start()
        across.append(copy)
        sends.append(copy)

    def to_y(k, j):
        row = d * n_code + flip(o, k)
        return remote(
            con_ref.at[row], con_ref.at[row], y_send.at[j, k], y_recv.at[j, k],
            (y + j) % n_y * 2 + core, o,
        )

    def held(k, j):
        return ((y + n_y - j) % n_y * 2 + core) * n_code + flip(o, k)

    def to_mate(k, j):
        row = held(k, j)
        return remote(
            con_ref.at[row], con_ref.at[row], c_send.at[j, k], c_recv.at[j, k], mate, o
        )

    if reply:
        acc[...] = jnp.zeros_like(acc)

    def absorb(row):
        if not reply:
            return
        here = con_ref[row, pl.ds(CBLK + 2, 1), :]

        def one(i, c):
            same = (asked_ref[i, pl.ds(0, 1), :].astype(jnp.float32) == here).astype(jnp.float32)
            acc[i] += con_ref[row] * same
            return c

        lax.fori_loop(0, n_code, one, 0)

    y_copies = {}
    mates = {}
    for k in range(n_code):
        if k == 0:
            own.wait()
        else:
            across[k - 1].wait_recv()
        for j in range(1, n_y):
            copy = to_y(k, j)
            copy.start()
            y_copies[j, k] = copy
            sends.append(copy)
        copy = to_mate(k, 0)
        copy.start()
        mates[0, k] = copy
        sends.append(copy)
        absorb(held(k, 0))
    for k in range(n_code):
        for j in range(1, n_y):
            y_copies[j, k].wait_recv()
            copy = to_mate(k, j)
            copy.start()
            mates[j, k] = copy
            sends.append(copy)
            absorb(held(k, j))
        mates[0, k].wait_recv()
        absorb(held(k, 0) + (1 - 2 * core) * n_code)
    for k in range(n_code):
        for j in range(1, n_y):
            mates[j, k].wait_recv()
            absorb(held(k, j) + (1 - 2 * core) * n_code)
    if reply:
        backs = []
        for k in range(n_code):
            peer = flip(o, k)
            for h in range(2):
                inv = 1.0 / (acc[peer, pl.ds(CBLK + h, 1), :] + 1.0)
                column = jnp.transpose(jnp.broadcast_to(inv, (128, 128)))
                rows = pl.ds(h * 128, 128)
                fresh = (acc[peer, rows, :] + served_ref[peer, rows, :]) * column
                if k == 0:
                    back_ref[o, rows, :] = fresh
                else:
                    stage[k, rows, :] = fresh
        for k in range(n_code - 1, 0, -1):
            copy = remote(
                stage.at[k], back_ref.at[o], b_send.at[k], b_recv.at[k], d, flip(o, k)
            )
            copy.start()
            backs.append(copy)
        for copy in backs:
            copy.wait()
    for copy in sends:
        copy.wait_send()


def sweeps_kernel(n_dp, n_code, key_blocks, block, own_blocks, feature, sweeps, *refs):
    slots_ref, counts_ref, want_ref, keys_ref, book_hbm = refs[:5]
    out_refs = refs[5 : 5 + sweeps]
    logsum_ref = refs[5 + sweeps]
    con_refs = refs[6 + sweeps : 6 + 2 * sweeps]
    (unnorm, peaks, run_top, run_total, words, norms, kst, kext, sums, acc, stage, served,
     fetched, back, asked, part, less, ids,
     id_send, id_recv, f_send, f_recv, b_send, b_recv,
     a_send, a_recv, y_send, y_recv, c_send, c_recv,
     book_sem, own_sem, smem_sem, out_sem, keep_sem) = refs[6 + 2 * sweeps :]
    scale = math.log2(math.e) / math.sqrt(feature)
    keys = key_blocks * block
    chunks = keys // 128
    d = lax.axis_index("dp")
    o = lax.axis_index("code")
    n_y = n_dp // 2
    y = d // 2
    core = d % 2
    mate = y * 2 + 1 - core
    far = n_code // 2

    def turn(k):
        out = o
        bit = 1
        while bit < n_code:
            out = out + bit * (k // bit % 2) * (1 - 2 * (o // bit % 2))
            bit *= 2
        return out

    barrier = pltpu.get_barrier_semaphore()
    for k in range(1, n_code):
        pl.semaphore_signal(barrier, inc=1, device_id=(d, flip(o, k)), device_id_type=MESH)
    for j in range(1, n_y):
        pl.semaphore_signal(
            barrier, inc=1, device_id=((y + j) % n_y * 2 + core, o), device_id_type=MESH
        )
    pl.semaphore_signal(barrier, inc=1, device_id=(mate, o), device_id_type=MESH)

    book = unnorm.at[n_code - 1]
    load = pltpu.make_async_copy(book_hbm, book.at[pl.ds(0, own_blocks)], book_sem)
    load.start()
    asked[0] = want_ref[o]
    own = pltpu.make_async_copy(want_ref.at[o], ids.at[0], smem_sem.at[0])
    own.start()
    pl.semaphore_wait(barrier, n_code - 1 + n_y - 1 + 1)

    asks = []
    for k in range(1, n_code):
        peer = flip(o, k)
        copy = remote(want_ref.at[peer], asked.at[k], id_send.at[k], id_recv.at[k], d, peer)
        copy.start()
        asks.append(copy)

    def gate(kb, c):
        count = counts_ref[kb]
        for k in range(n_code):
            slot = turn(k)
            hit = jnp.float32(1e30)
            for l in range(LIST_MAX):
                same = (lax.div(slots_ref[kb, l], own_blocks) == slot) & (count > l)
                hit = jnp.where(same, jnp.float32(0.0), hit)
            less[kb, k] = hit
        return c

    def serve_copy(k):
        peer = flip(o, k)
        return remote(served.at[k], fetched.at[k], f_send.at[k], f_recv.at[k], d, peer)

    def move(k):
        return pltpu.make_async_copy(asked.at[k], ids.at[k], smem_sem.at[k])

    load.wait()
    own.wait()
    first = unnorm[n_code - 1, ids[0, 0, 0]]
    served[0] = first
    fetched[0] = first
    serves = []
    for k in range(1, n_code + 1):
        if k < n_code:
            asks[k - 1].wait_recv()
            move(k).start()
        if k > 1:
            move(k - 1).wait()
            served[k - 1] = unnorm[n_code - 1, ids[k - 1, 0, 0]]
            copy = serve_copy(k - 1)
            copy.start()
            serves.append(copy)

    kext[:, 128:256] = jnp.ones((keys, 128), jnp.bfloat16)
    kext[:, 0:128] = keys_ref[...]

    def turn_keys(c, carry):
        at = pl.ds(pl.multiple_of(c * block, block), block)
        turned = jnp.transpose(keys_ref[at, :])
        kst[0:128, at] = turned
        kst[128:256, at] = turned
        return carry

    lax.fori_loop(0, key_blocks, turn_keys, 0)
    lax.fori_loop(0, key_blocks, gate, 0)

    def score(k, blocks):
        value = blocks[k]
        scaled = value * scale
        hi = scaled.astype(jnp.bfloat16)
        words[:, 0:128] = hi
        words[:, 128:256] = (scaled - hi.astype(jnp.float32)).astype(jnp.bfloat16)
        half = (0.5 * scale) * jnp.sum(value * value, axis=1, keepdims=True)
        norms[...] = jnp.broadcast_to(half, (CBLK, 128))

        def some(i, c):
            for u in range(8):
                q = i * 8 + u
                cols = pl.ds(pl.multiple_of(q * 256, 256), 256)
                right = kst[:, cols]
                away = less[q * 256 // block, k]
                tops, parts = [], []
                for h in range(2):
                    rows = slice(h * 128, (h + 1) * 128)
                    raw = jnp.dot(words[rows, :], right, preferred_element_type=jnp.float32)
                    s = raw - jnp.tile(norms[rows, :], (1, 2))
                    s = s.reshape(16, 8, 256)
                    top = jnp.max(s, axis=0)
                    e = jnp.exp2(s - top[None])
                    peaks[k, h, :, cols] = top
                    tops.append(top - away)
                    parts.append(jnp.sum(e, axis=0))
                    e = e.reshape(128, 256)
                    unnorm[k, 2 * q, rows, :] = e[:, 0:128]
                    unnorm[k, 2 * q + 1, rows, :] = e[:, 128:256]
                old = run_top[:, cols]
                new = jnp.maximum(old, jnp.maximum(tops[0], tops[1]))
                run_top[:, cols] = new
                run_total[:, cols] = run_total[:, cols] * jnp.exp2(old - new) + (
                    parts[0] * jnp.exp2(tops[0] - new) + parts[1] * jnp.exp2(tops[1] - new)
                )
            return c

        lax.fori_loop(0, keys // 256 // 8, some, 0)

    def normalise(last):
        def one(kb, c):
            cols = pl.ds(pl.multiple_of(kb * block, block), block)
            top = run_top[:, cols]
            peak = jnp.max(top, axis=0, keepdims=True)
            total = jnp.sum(run_total[:, cols] * jnp.exp2(top - peak), axis=0, keepdims=True)
            if last:
                row = peak * math.log(2.0) + jnp.log(total)
                for i in range(block // 128):
                    at = pl.ds(kb * (block // 128) + i, 1)
                    logsum_ref[at, :] = row[:, i * 128 : (i + 1) * 128]
            run_top[:, cols] = jnp.broadcast_to(peak, (8, block))
            run_total[:, cols] = jnp.broadcast_to(1.0 / total, (8, block))
            return c

        lax.fori_loop(0, key_blocks, one, 0)

    def collect(k):
        total = None
        for q in range(keys // 512):
            halves = []
            for h in range(2):
                rows = slice(h * 128, (h + 1) * 128)
                tiles = []
                for u in range(4):
                    e = unnorm[k, q * 4 + u, rows, :].reshape(16, 8, 128)
                    cols = pl.ds((q * 4 + u) * 128, 128)
                    w = (peaks[k, h, :, cols] - less[q * 512 // block, k]) - run_top[:, cols]
                    w = jnp.exp2(w) * run_total[:, cols]
                    tiles.append((e * w[None]).reshape(128, 128).astype(jnp.bfloat16))
                halves.append(jnp.concatenate(tiles, axis=1))
            piece = jnp.dot(
                jnp.concatenate(halves, axis=0), kext[q * 512 : (q + 1) * 512, :],
                preferred_element_type=jnp.float32,
            )
            total = piece if total is None else total + piece
        part[...] = total
        for h in range(2):
            turned = jnp.transpose(part[h * 128 : (h + 1) * 128, 128:256])
            sums[k, CBLK + h : CBLK + h + 1, :] = turned[0:1, :]
        sums[k, CBLK + 2 :, :] = want_ref[turn(k), 2:, :].astype(jnp.float32)
        sums[k, :CBLK, :] = part[:, 0:128]

    def held(k, j):
        return ((y + n_y - j) % n_y * 2 + core) * n_code + turn(k)

    keeps = []
    wide = list(range(far, n_code))
    close = list(range(2, far))
    beside = list(range(1, min(2, far)))
    beside = list(range(1, min(2, far)))
    inner = wide[:1] + close + wide[1:2] + [0] + beside + wide[2:]
    outer = close + [0] + wide[:1] + beside + wide[1:]
    inner_in = close + wide[:2] + beside + wide[2:]
    outer_in = beside + wide[:1] + wide[2:] + close[:1] + wide[1:2] + close[1:]
    middle = (o // far % 2) != (o // max(far // 2, 1) % 2)

    def choose(i, first, second):
        return jnp.where(middle, first[i], second[i])

    def table(p, first, second):
        out = choose(0, first, second)
        for i in range(1, n_code):
            out = jnp.where(p == i, choose(i, first, second), out)
        return out

    def pick(p):
        return table(p, inner, outer)

    waits = [("y", i) for i in range(n_code)]
    events = [("a", i) for i in range(min(far, n_code - 1))]
    for i in range(len(events), n_code - 1):
        take = 2 if i < n_code - 2 else 1
        events += waits[:take] + [("a", i)]
        waits = waits[take:]
    events += waits

    def serve_copy_at(k):
        return remote(served.at[k], fetched.at[k], f_send.at[k], f_recv.at[k], d, turn(k))

    def back_copy_at(k):
        return remote(stage.at[k], back.at[k], b_send.at[k], b_recv.at[k], d, turn(k))

    for sweep in range(sweeps):
        reply = sweep + 1 < sweeps
        con_ref = con_refs[sweep]
        blocks = fetched if sweep == 0 else back

        run_top[...] = jnp.full((8, keys), -3e38, jnp.float32)
        run_total[...] = jnp.zeros((8, keys), jnp.float32)

        def scoring(k, c):
            @pl.when(k > 0)
            def _():
                if sweep == 0:
                    serve_copy_at(k).wait_recv()
                else:
                    back_copy_at(k).wait_recv()

            score(k, blocks)
            return c

        lax.fori_loop(0, n_code, scoring, 0)
        normalise(not reply)

        def across(k):
            return remote(
                sums.at[k], con_ref.at[d * n_code + o],
                a_send.at[sweep, k], a_recv.at[sweep, k], d, turn(k),
            )

        def to_y(k, j):
            row = held(k, 0)
            return remote(
                con_ref.at[row], con_ref.at[row],
                y_send.at[sweep, j, k], y_recv.at[sweep, j, k],
                (y + j) % n_y * 2 + core, o,
            )

        def own_y(j):
            return remote(
                sums.at[0], con_ref.at[d * n_code + o],
                y_send.at[sweep, j, 0], y_recv.at[sweep, j, 0],
                (y + j) % n_y * 2 + core, o,
            )

        def own_mate():
            return remote(
                sums.at[0], con_ref.at[d * n_code + o],
                c_send.at[sweep, 0, 0], c_recv.at[sweep, 0, 0], mate, o,
            )

        def to_mate(k, j):
            row = held(k, j)
            return remote(
                con_ref.at[row], con_ref.at[row],
                c_send.at[sweep, j, k], c_recv.at[sweep, j, k], mate, o,
            )

        if reply:
            acc[...] = jnp.zeros_like(acc)

        def absorb(row):
            if not reply:
                pltpu.make_async_copy(
                    con_ref.at[row], out_refs[sweep].at[row], out_sem.at[row]
                ).start()
                return
            here = con_ref[row, pl.ds(CBLK + 2, 1), :]

            def one(i, c):
                same = (asked[i, pl.ds(0, 1), :].astype(jnp.float32) == here).astype(jnp.float32)
                acc[i] += con_ref[row] * same
                return c

            lax.fori_loop(0, n_code, one, 0)

        mine = pltpu.make_async_copy(sums.at[0], con_ref.at[d * n_code + o], own_sem)

        def depart(k):
            @pl.when(k > 0)
            def _():
                across(k).start()

            @pl.when(k == 0)
            def _():
                mine.start()
                for j in range(1, n_y):
                    own_y(j).start()
                own_mate().start()

        def produce(p, c):
            collect(pick(p))

            @pl.when(p > 0)
            def _():
                depart(pick(p - 1))

            return c

        lax.fori_loop(0, n_code, produce, 0)
        mine.wait()
        depart(pick(n_code - 1))
        absorb(held(0, 0))
        for kind, i in events:
            if kind == "a":
                k = choose(i, inner_in, outer_in)
                across(k).wait_recv()
                for j in range(1, n_y):
                    to_y(k, j).start()
                to_mate(k, 0).start()
                absorb(held(k, 0))
            else:
                k = choose(i - 1, inner_in, outer_in) if i else 0
                for j in range(1, n_y):
                    to_y(k, j).wait_recv()
                    to_mate(k, j).start()
                    absorb(held(k, j))
                to_mate(k, 0).wait_recv()
                absorb(held(k, 0) + (1 - 2 * core) * n_code)
        for i in range(n_code):
            k = choose(i - 1, inner_in, outer_in) if i else 0
            for j in range(1, n_y):
                to_mate(k, j).wait_recv()
                absorb(held(k, j) + (1 - 2 * core) * n_code)
        for k in range(1, n_code):
            across(k).wait_send()
        for k in range(n_code):
            for j in range(1, n_y):
                to_y(k, j).wait_send()
                to_mate(k, j).wait_send()
            to_mate(k, 0).wait_send()
        if reply:
            for p in range(n_code):
                k = (p + 1) % n_code
                for h in range(2):
                    inv = 1.0 / (acc[k, pl.ds(CBLK + h, 1), :] + 1.0)
                    column = jnp.transpose(jnp.broadcast_to(inv, (128, 128)))
                    rows = pl.ds(h * 128, 128)
                    fresh = (acc[k, rows, :] + served[k, rows, :]) * column
                    if k == 0:
                        back[0, rows, :] = fresh
                    else:
                        stage[k, rows, :] = fresh
                if p > 0:
                    back_copy_at(p).start()
            keep = pltpu.make_async_copy(con_ref, out_refs[sweep], keep_sem.at[sweep])
            keep.start()
            keeps.append(keep)
    for row in range(n_dp * n_code):
        pltpu.make_async_copy(
            con_refs[-1].at[row], out_refs[-1].at[row], out_sem.at[row]
        ).wait()
    for k in range(1, n_code):
        back_copy_at(k).wait_send()
    for keep in keeps:
        keep.wait()
    for copy in asks + serves:
        copy.wait_send()


def finish_kernel(n, own_blocks, sweeps, *refs):
    con_hbm = refs[:sweeps]
    book_hbm, out_hbm = refs[sweeps : sweeps + 2]
    con, total, mass, ids, con_sem, book_sem, out_sem = refs[sweeps + 2 :]
    book = pltpu.make_async_copy(book_hbm, total, book_sem)
    book.start()
    half = n // 2

    def load(t, h):
        rows = pl.ds(h * half, half)
        return pltpu.make_async_copy(con_hbm[t].at[rows], con.at[rows], con_sem.at[h])

    load(0, 0).start()
    load(0, 1).start()
    outs = []
    for t in range(sweeps):
        mass[...] = jnp.ones_like(mass)
        for h in range(2):
            load(t, h).wait()
            if t == 0:

                def name(j, c):
                    for u in range(8):
                        i = j * 8 + u
                        ids[i] = jnp.max(con[i, pl.ds(CBLK + 2, 1), :]).astype(jnp.int32)
                    return c

                lax.fori_loop(h * half // 8, (h + 1) * half // 8, name, 0)
                if h == 0:
                    book.wait()

            def add(j, c):
                b = ids[j]
                total[b] += con[j, :CBLK, :]
                for g in range(2):
                    row = pl.ds(g * (mass.shape[0] // 2) + b, 1)
                    mass[row, :] += con[j, pl.ds(CBLK + g, 1), :]
                return c

            lax.fori_loop(h * half, (h + 1) * half, add, 0)
            if t + 1 < sweeps:
                load(t + 1, h).start()
        columns = jnp.transpose(1.0 / mass[...])
        for b in range(own_blocks):
            for g in range(2):
                lane = g * (mass.shape[0] // 2) + b
                total[b, g * 128 : (g + 1) * 128, :] = (
                    total[b, g * 128 : (g + 1) * 128, :] * columns[:, lane : lane + 1]
                )
            if t + 1 == sweeps:
                out = pltpu.make_async_copy(total.at[b], out_hbm.at[b], out_sem.at[b])
                out.start()
                outs.append(out)
    for out in outs:
        out.wait()


def assign_kernel(
    n_slots, key_blocks, block, feature,
    slots_ref, counts_ref, fetched_ref, keys_ref, want_ref,
    sums_ref, logsum_ref,
    words, norms, kst, kext, picked, scores, post, acc,
):
    scale = math.log2(math.e) / math.sqrt(feature)

    for s in range(n_slots):
        value = fetched_ref[s]
        scaled = value * scale
        hi = scaled.astype(jnp.bfloat16)
        words[s, :, 0:128] = hi
        words[s, :, 128:256] = (scaled - hi.astype(jnp.float32)).astype(jnp.bfloat16)
        half = (0.5 * scale) * jnp.sum(value * value, axis=1, keepdims=True)
        norms[s] = jnp.broadcast_to(half, (CBLK, 128))
        acc[s] = jnp.zeros((CBLK, 256), jnp.float32)
    kext[:, 128:256] = jnp.ones((block, 128), jnp.bfloat16)

    def key_block(kb, c):
        keys = keys_ref[pl.ds(pl.multiple_of(kb * block, block), block), :]
        kext[:, 0:128] = keys
        turned = jnp.transpose(keys)
        kst[0:128, :] = turned
        kst[128:256, :] = turned
        count = counts_ref[kb]
        slots = [slots_ref[kb, l] for l in range(LIST_MAX)]
        for l in range(LIST_MAX):
            picked[l * CBLK : (l + 1) * CBLK, :] = words[slots[l]]
        raw = jnp.dot(picked[...], kst[...], preferred_element_type=jnp.float32)
        top = jnp.full((8, block), -3e38, jnp.float32)
        for l in range(LIST_MAX):
            rows = slice(l * CBLK, (l + 1) * CBLK)
            less = norms[slots[l]] + jnp.where(l < count, 0.0, 1e30)
            s = raw[rows] - jnp.tile(less, (1, block // 128))
            scores[rows, :] = s
            top = jnp.maximum(top, jnp.max(s.reshape(CBLK // 8, 8, block), axis=0))
        peak = jnp.max(top, axis=0, keepdims=True)
        total = jnp.zeros((8, block), jnp.float32)
        for l in range(LIST_MAX):
            rows = slice(l * CBLK, (l + 1) * CBLK)
            e = jnp.exp2(scores[rows, :] - peak)
            scores[rows, :] = e
            total = total + jnp.sum(e.reshape(CBLK // 8, 8, block), axis=0)
        total = jnp.sum(total, axis=0, keepdims=True)
        logsum_ref[kb] = peak * math.log(2.0) + jnp.log(total)
        inv = 1.0 / total
        post[...] = (scores[...] * inv).astype(jnp.bfloat16)
        weighted = jnp.dot(post[...], kext[...], preferred_element_type=jnp.float32)
        for l in range(LIST_MAX):
            acc[slots[l]] += weighted[l * CBLK : (l + 1) * CBLK]
        return c

    lax.fori_loop(0, key_blocks, key_block, 0)

    for s in range(n_slots):
        sums_ref[s, :CBLK, :] = acc[s, :, 0:128]
        for h in range(2):
            turned = jnp.transpose(acc[s, h * 128 : (h + 1) * 128, 128:256])
            sums_ref[s, CBLK + h : CBLK + h + 1, :] = turned[0:1, :]
        sums_ref[s, CBLK + 2 :, :] = want_ref[s, 2:, :].astype(jnp.float32)


def on_device(cached_keys, codebook, block_lists, counts):
    n_dp = lax.axis_size("dp")
    n_code = lax.axis_size("code")
    n = n_dp * n_code
    own_rows, feature = codebook.shape
    own_blocks = own_rows // CBLK
    key_blocks = block_lists.shape[0]
    block = cached_keys.shape[0] // key_blocks
    f32 = jnp.float32
    dma = pltpu.SemaphoreType.DMA

    slots = block_lists // own_blocks
    local = block_lists % own_blocks
    wanted = jnp.max(
        jnp.where(
            slots.reshape(-1)[:, None] == jnp.arange(128)[None, :], local.reshape(-1)[:, None], 0
        ),
        axis=0,
    )
    want = jnp.broadcast_to(wanted[:n_code, None, None], (n_code, 8, 128)).astype(jnp.int32)
    blocks = jax.ShapeDtypeStruct((n_code, CBLK, feature), f32)
    sums_shape = jax.ShapeDtypeStruct((n_code, CBLK + MROWS, feature), f32)
    con_shape = jax.ShapeDtypeStruct((n, CBLK + MROWS, feature), f32)
    n_y = n_dp // 2

    def params(**kw):
        return pltpu.CompilerParams(vmem_limit_bytes=VLIMIT, **kw)

    book = codebook.reshape(own_blocks, CBLK, feature)

    def finish(parts, held):
        return pl.pallas_call(
            functools.partial(finish_kernel, n, own_blocks, len(parts)),
            out_shape=jax.ShapeDtypeStruct((own_blocks, CBLK, feature), f32),
            in_specs=[ANY] * (len(parts) + 1),
            out_specs=ANY,
            scratch_shapes=[
                pltpu.VMEM(con_shape.shape, f32),
                pltpu.VMEM((own_blocks, CBLK, feature), f32),
                pltpu.VMEM((max(128, 2 * own_blocks), 128), f32),
                pltpu.SMEM((n,), jnp.int32),
                dma((2,)), dma, dma((own_blocks,)),
            ],
            compiler_params=params(),
        )(*parts, held)

    keys = key_blocks * block
    joint = (
        ITERS * n * (CBLK + MROWS) * feature * 4 <= HELD_BYTES
        and own_blocks * 128 <= keys
        and n_code * CBLK * keys * 4 <= HELD_BYTES * 2 + HELD_BYTES // 2
        and keys % 2048 == 0 and block % 512 == 0
    )
    if joint:
        bf16 = jnp.bfloat16
        results = pl.pallas_call(
            functools.partial(
                sweeps_kernel, n_dp, n_code, key_blocks, block, own_blocks, feature, ITERS
            ),
            out_shape=(con_shape,) * ITERS
            + (jax.ShapeDtypeStruct((keys // 128, 128), f32),),
            in_specs=[SM, SM, VM, VM, ANY],
            out_specs=(ANY,) * ITERS + (VM,),
            scratch_shapes=[pltpu.VMEM(con_shape.shape, f32) for _ in range(ITERS)] + [
                pltpu.VMEM((n_code, keys // 128, CBLK, 128), f32),
                pltpu.VMEM((n_code, 2, 8, keys), f32),
                pltpu.VMEM((8, keys), f32),
                pltpu.VMEM((8, keys), f32),
                pltpu.VMEM((CBLK, 256), bf16),
                pltpu.VMEM((CBLK, 128), f32),
                pltpu.VMEM((256, keys), bf16),
                pltpu.VMEM((keys, 256), bf16),
                pltpu.VMEM(sums_shape.shape, f32),
                pltpu.VMEM(sums_shape.shape, f32),
                pltpu.VMEM(blocks.shape, f32),
                pltpu.VMEM(blocks.shape, f32),
                pltpu.VMEM(blocks.shape, f32),
                pltpu.VMEM(blocks.shape, f32),
                pltpu.VMEM((n_code, 8, 128), jnp.int32),
                pltpu.VMEM((CBLK, 256), f32),
                pltpu.SMEM((key_blocks, n_code), f32),
                pltpu.SMEM((n_code, 8, 128), jnp.int32),
                dma((n_code,)), dma((n_code,)),
                dma((n_code,)), dma((n_code,)),
                dma((n_code,)), dma((n_code,)),
                dma((ITERS, n_code)), dma((ITERS, n_code)),
                dma((ITERS, n_y, n_code)), dma((ITERS, n_y, n_code)),
                dma((ITERS, n_y, n_code)), dma((ITERS, n_y, n_code)),
                dma, dma, dma((n_code,)), dma((n,)), dma((ITERS,)),
            ],
            compiler_params=params(collective_id=0, has_side_effects=True),
        )(block_lists, counts, want, cached_keys, book)
        current = finish(results[:ITERS], book)
        return (current.reshape(own_rows, feature), results[ITERS].reshape(-1))

    fetched, served, asked = pl.pallas_call(
        functools.partial(fetch_kernel, n_code),
        out_shape=(blocks, blocks, jax.ShapeDtypeStruct((n_code, 8, 128), jnp.int32)),
        in_specs=[VM, ANY],
        out_specs=(VM, VM, VM),
        scratch_shapes=[
            pltpu.VMEM((own_blocks, CBLK, feature), f32),
            pltpu.SMEM((n_code, 8, 128), jnp.int32),
            dma((n_code,)), dma((n_code,)), dma((n_code,)), dma((n_code,)),
            dma, dma, dma((n_code,)),
        ],
        compiler_params=params(collective_id=0, has_side_effects=True),
    )(want, book)
    current = book
    for sweep in range(ITERS):
        reply = sweep + 1 < ITERS
        sems = [
            dma((n_code,)), dma((n_code,)),
            dma((n_y, n_code)), dma((n_y, n_code)),
            dma((n_y, n_code)), dma((n_y, n_code)),
            dma,
        ]
        sums, logsum = pl.pallas_call(
            functools.partial(assign_kernel, n_code, key_blocks, block, feature),
            out_shape=(sums_shape, jax.ShapeDtypeStruct((key_blocks, 1, block), f32)),
            in_specs=[SM, SM, VM, VM, VM],
            out_specs=(VM, VM),
            scratch_shapes=[
                pltpu.VMEM((n_code, CBLK, 256), jnp.bfloat16),
                pltpu.VMEM((n_code, CBLK, 128), f32),
                pltpu.VMEM((256, block), jnp.bfloat16),
                pltpu.VMEM((block, 256), jnp.bfloat16),
                pltpu.VMEM((LIST_MAX * CBLK, 256), jnp.bfloat16),
                pltpu.VMEM((LIST_MAX * CBLK, block), f32),
                pltpu.VMEM((LIST_MAX * CBLK, block), jnp.bfloat16),
                pltpu.VMEM((n_code, CBLK, 256), f32),
            ],
            compiler_params=params(),
        )(slots, counts, fetched, cached_keys, want)
        if reply:
            con, fetched = pl.pallas_call(
                functools.partial(exchange_kernel, n_dp, n_code, True),
                out_shape=(con_shape, blocks),
                in_specs=[VM, VM, VM],
                out_specs=(VM, VM),
                scratch_shapes=[
                    pltpu.VMEM(sums_shape.shape, f32), pltpu.VMEM(blocks.shape, f32)
                ] + sems + [dma((n_code,)), dma((n_code,))],
                compiler_params=params(collective_id=1 + sweep, has_side_effects=True),
            )(sums, served, asked)
        else:
            con = pl.pallas_call(
                functools.partial(exchange_kernel, n_dp, n_code, False),
                out_shape=con_shape,
                in_specs=[VM],
                out_specs=VM,
                scratch_shapes=sems,
                compiler_params=params(collective_id=1 + sweep, has_side_effects=True),
            )(sums)
        current = finish([con], current)
        if reply:
            current, fetched = lax.optimization_barrier((current, fetched))
    return (current.reshape(own_rows, feature), logsum.reshape(-1))


def solution(mesh):
    in_specs = (
        P(("dp", "code"), None),
        P("code", None),
        P(("dp", "code"), None),
        P(("dp", "code")),
    )
    out_specs = (P("code", None), P(("dp", "code")))
    return jax.shard_map(
        on_device, mesh=mesh, in_specs=in_specs, out_specs=out_specs, check_vma=False
    )
```
